256 devices in a mesh: ctx: 32 (over x, z), ch: 8 (over y, core).
Axes of the slice: x: 4, y: 4, z: 8, core: 2. Of those that a mesh axis runs over, the one named last changes fastest.
Arguments:
- query_gate: bfloat16 [16384, 4096], P('ctx', 'ch'), may hold values from -6 to 6
- key_gate: bfloat16 [16384, 4096], P('ctx', 'ch'), may hold values from -6 to 6
- value_in: bfloat16 [16384, 4096], P('ctx', 'ch'), may hold values from -6 to 6
- filter_taps: float32 [4096, 4096], P(None, 'ch'), may hold values from -0.09375 to 0.09375
- skip_gain: float32 [4096], P('ch'), may hold values from -4 to 4
- out_weight: bfloat16 [4096, 4096], P('ch'), may hold values from -0.09375 to 0.09375
Outputs:
- mixed_out: bfloat16 [16384, 4096], P('ctx', 'ch')
The draws below stay inside these ranges and needn't reach their ends.
All inputs are finite; a program needn't handle non-finite values.
Results may differ from the reference program's by a relative error of at most 0.017.
Values may be sent and summed in bfloat16 or wider, within the bound.
No kernel may reach another device: no remote copies, remote signals or barrier semaphores. Data moves between devices by JAX's collectives and lax.ppermute only.
A program may use at most 128 MiB of HBM per device.

```python
import jax
import jax.numpy as jnp
from jax import lax

D = 4096
SPAN = 512
WIN = 8
SEQ = 16384
N_CTX = 32


def levels(rng, shape, shards, smallest, largest):
    level, own = 1.0, jax.random.fold_in(rng, 6)
    for dim, shards_of in shards:
        draws = jnp.exp(jax.random.uniform(jax.random.fold_in(own, dim), (shards_of,), jnp.float32, smallest / len(shards), largest / len(shards)))
        level = level * jnp.repeat(draws, shape[dim] // shards_of).reshape([-1 if axis == dim else 1 for axis in range(len(shape))])
    return level


def noise(rng, extent, deviation, bound, pieces=(), held_as=jnp.bfloat16):
    entries = jax.random.normal(rng, extent, jnp.float32) * deviation
    if len(pieces) > 0:
        entries = levels(rng, extent, pieces, -0.22, 0.18) * entries
    return jnp.clip(entries, min=-bound, max=bound).astype(held_as)


def setup_inputs(seed: int = 0) -> dict:
    arg_keys = jax.random.split(jax.random.key(seed), 7)
    query_gate = noise(arg_keys[0], (SEQ, D), 1.0, 6.0, ((0, 32), (1, 8)))
    key_gate = noise(arg_keys[1], (SEQ, D), 1.0, 6.0, ((0, 32), (1, 8)))
    value_in = noise(arg_keys[2], (SEQ, D), 1.0, 6.0, ((0, 32), (1, 8)))
    filter_taps = noise(arg_keys[3], (WIN * SPAN, D), (WIN * SPAN) ** -0.5, 0.09375, ((1, 8),), jnp.float32)
    skip_gain = noise(arg_keys[4], (D,), 1.0, 4.0, ((0, 8),), jnp.float32)
    out_weight = noise(arg_keys[5], (D, D), D ** -0.5, 0.09375, ((0, 8),))
    return dict(query_gate=query_gate, key_gate=key_gate, value_in=value_in, filter_taps=filter_taps, skip_gain=skip_gain, out_weight=out_weight)


def reference(query_gate, key_gate, value_in, filter_taps, skip_gain, out_weight):
    mixed_in = (key_gate.astype(jnp.float32) * value_in.astype(jnp.float32)).astype(jnp.bfloat16)
    spans = mixed_in.astype(jnp.float32).reshape(N_CTX, SPAN, D)
    spectra = jnp.fft.rfft(spans, n=2 * SPAN, axis=1)
    real_part = lax.optimization_barrier(jnp.real(spectra).astype(jnp.bfloat16)).astype(jnp.float32)
    imag_part = lax.optimization_barrier(jnp.imag(spectra).astype(jnp.bfloat16)).astype(jnp.float32)
    padded_taps = jnp.concatenate([jnp.zeros((SPAN, D), jnp.float32), filter_taps, jnp.zeros((SPAN, D), jnp.float32)], axis=0)
    leading = jnp.zeros((WIN, SPAN + 1, D), jnp.float32)
    real_padded = jnp.concatenate([leading, real_part], axis=0)
    imag_padded = jnp.concatenate([leading, imag_part], axis=0)
    total_real = jnp.zeros((N_CTX, SPAN + 1, D), jnp.float32)
    total_imag = jnp.zeros((N_CTX, SPAN + 1, D), jnp.float32)
    for lag_index in range(WIN + 1):
        window = padded_taps[lag_index * SPAN: lag_index * SPAN + 2 * SPAN]
        kernel = jnp.fft.rfft(window, axis=0)
        kernel_real = jnp.real(kernel)[None]
        kernel_imag = jnp.imag(kernel)[None]
        shifted_real = real_padded[WIN - lag_index: WIN - lag_index + N_CTX]
        shifted_imag = imag_padded[WIN - lag_index: WIN - lag_index + N_CTX]
        total_real = total_real + kernel_real * shifted_real - kernel_imag * shifted_imag
        total_imag = total_imag + kernel_real * shifted_imag + kernel_imag * shifted_real
    signal = jnp.fft.irfft(lax.complex(total_real, total_imag), n=2 * SPAN, axis=1)
    conv_out = signal[:, SPAN:, :].reshape(SEQ, D)
    combined = conv_out + skip_gain[None, :] * mixed_in.astype(jnp.float32)
    gated = (query_gate.astype(jnp.float32) * combined).astype(jnp.bfloat16)
    return jnp.dot(gated, out_weight, preferred_element_type=jnp.float32).astype(jnp.bfloat16)
```

```python
import functools

import jax
import jax.numpy as jnp
import numpy as np
from jax import lax
from jax.experimental import pallas as pl
from jax.experimental.pallas import tpu as pltpu
from jax.sharding import PartitionSpec as P

WIN = 8
LANES = 128
CORES = 2


def odd_tables(length):
    order = np.concatenate([np.arange(0, length, 2), np.arange(1, length, 2)])
    turns = (np.arange(length)[:, None] * (2 * order[None, :] + 1)) % (4 * length)
    angle = turns * (np.pi / (2 * length))
    tiles = length // LANES
    cos_part = np.cos(angle).reshape(length, tiles, LANES)
    sin_part = -np.sin(angle).reshape(length, tiles, LANES)
    table = np.concatenate([cos_part, sin_part], axis=2).transpose(1, 0, 2)
    return table.astype(jnp.bfloat16)


def mix_kernel(key_ref, value_ref, mixed_ref, turned_ref):
    product = (key_ref[...].astype(jnp.float32) * value_ref[...].astype(jnp.float32)).astype(jnp.bfloat16)
    mixed_ref[...] = product
    turned_ref[...] = product.T


def mix(key_gate, value_in):
    length, width = key_gate.shape
    return pl.pallas_call(
        mix_kernel,
        grid=(width // LANES,),
        in_specs=[pl.BlockSpec((length, LANES), lambda i: (0, i))] * 2,
        out_specs=[
            pl.BlockSpec((length, LANES), lambda i: (0, i)),
            pl.BlockSpec((LANES, length), lambda i: (i, 0)),
        ],
        out_shape=[
            jax.ShapeDtypeStruct((length, width), jnp.bfloat16),
            jax.ShapeDtypeStruct((width, length), jnp.bfloat16),
        ],
        cost_estimate=pl.CostEstimate(flops=length * width, bytes_accessed=8 * length * width, transcendentals=0),
        name="mix",
    )(key_gate, value_in)


def taps_kernel(few, place_ref, taps_ref, table_ref, out_ref, turned):
    step = pl.program_id(0)
    length = table_ref.shape[1]
    first = place_ref[1] * few
    rows = lax.broadcasted_iota(jnp.int32, (few, LANES), 0)
    lanes = lax.broadcasted_iota(jnp.int32, (few, LANES), 1)
    pick = (lanes == rows + first).astype(jnp.bfloat16)
    picked = lax.dot_general(
        pick, taps_ref[...].astype(jnp.bfloat16), (((1,), (1,)), ((), ())), preferred_element_type=jnp.float32
    ).astype(jnp.bfloat16)
    for half in range(2):
        start = pl.multiple_of((2 * step + half) * few, few)
        turned[pl.ds(start, few), :] = picked[:, half * length : (half + 1) * length]

    @pl.when(step == pl.num_programs(0) - 1)
    def _():
        for tile in range(table_ref.shape[0]):
            out_ref[tile] = jnp.dot(turned[...], table_ref[tile], preferred_element_type=jnp.float32)


def taps_spectrum(place, filter_taps, table, few):
    tiles, length, pair = table.shape
    rows = WIN * few
    return pl.pallas_call(
        functools.partial(taps_kernel, few),
        grid_spec=pltpu.PrefetchScalarGridSpec(
            num_scalar_prefetch=1,
            grid=(WIN // 2,),
            in_specs=[
                pl.BlockSpec((2 * length, LANES), lambda i, place: (i, place[0])),
                pl.BlockSpec((tiles, length, pair), lambda i, place: (0, 0, 0)),
            ],
            out_specs=pl.BlockSpec((tiles, rows, pair), lambda i, place: (0, 0, 0)),
            scratch_shapes=[pltpu.VMEM((rows, length), jnp.bfloat16)],
        ),
        out_shape=jax.ShapeDtypeStruct((tiles, rows, pair), jnp.float32),
        cost_estimate=pl.CostEstimate(
            flops=2 * rows * length * tiles * pair, bytes_accessed=3 << 20, transcendentals=0
        ),
        name="taps_spectrum",
    )(place, filter_taps, table)


def conv_kernel(few, x_ref, h_ref, table_ref, out_ref, window, total, product, gathered):
    tile = pl.program_id(0)
    tiles = pl.num_programs(0)
    count, length = x_ref.shape
    spans = count // few
    spectrum = jnp.dot(x_ref[...], table_ref[0], preferred_element_type=jnp.float32)
    real, imag = spectrum[:, :LANES], spectrum[:, LANES:]
    sign = jnp.where(tile < tiles // 2, 1.0, -1.0).astype(jnp.float32)
    zero = jnp.zeros((few, LANES), jnp.float32)
    before_real = jnp.concatenate([zero, real[:-few]], axis=0)
    before_imag = jnp.concatenate([zero, imag[:-few]], axis=0)
    window_real = before_real + sign * imag
    window_imag = before_imag - sign * real
    window[0] = window_real
    window[1] = window_imag
    window[2] = window_real + window_imag
    for part in range(few // 8):
        low = part * 8
        first, plus, minus = [], [], []
        for lag in range(WIN):
            h_real = h_ref[0, lag * few + low : lag * few + low + 8, :LANES]
            h_imag = h_ref[0, lag * few + low : lag * few + low + 8, LANES:]
            first.append(h_real)
            plus.append(h_real + h_imag)
            minus.append(h_imag - h_real)
        for span in range(spans):
            one = two = three = None
            for lag in range(min(WIN, span + 1)):
                at = (span - lag) * few + low
                term_one = first[lag] * window[2, at : at + 8, :]
                term_two = plus[lag] * window[1, at : at + 8, :]
                term_three = minus[lag] * window[0, at : at + 8, :]
                one = term_one if one is None else one + term_one
                two = term_two if two is None else two + term_two
                three = term_three if three is None else three + term_three
            at = span * few + low
            total[0, at : at + 8, :] = one + three
            total[1, at : at + 8, :] = one - two
    scale = sign * (1.0 / length)
    product[:, :LANES] = (-scale * total[0]).astype(jnp.bfloat16)
    product[:, LANES:] = (scale * total[1]).astype(jnp.bfloat16)
    part_out = lax.dot_general(
        product[...], table_ref[0], (((1,), (1,)), ((), ())), preferred_element_type=jnp.float32
    )

    @pl.when(tile == 0)
    def _():
        gathered[...] = part_out

    @pl.when(tile > 0)
    def _():
        gathered[...] += part_out

    @pl.when(tile == tiles - 1)
    def _():
        out_ref[...] = gathered[...].astype(jnp.bfloat16)


def convolve(turned, spectrum, table, few):
    count, length = turned.shape
    tiles, _, pair = table.shape
    rows = WIN * few
    return pl.pallas_call(
        functools.partial(conv_kernel, few),
        grid=(tiles,),
        in_specs=[
            pl.BlockSpec((count, length), lambda i: (0, 0)),
            pl.BlockSpec((1, rows, pair), lambda i: (i, 0, 0)),
            pl.BlockSpec((1, length, pair), lambda i: (i, 0, 0)),
        ],
        out_specs=pl.BlockSpec((count, length), lambda i: (0, 0)),
        out_shape=jax.ShapeDtypeStruct((count, length), jnp.bfloat16),
        scratch_shapes=[
            pltpu.VMEM((3, count, LANES), jnp.float32),
            pltpu.VMEM((2, count, LANES), jnp.float32),
            pltpu.VMEM((count, pair), jnp.bfloat16),
            pltpu.VMEM((count, length), jnp.float32),
        ],
        cost_estimate=pl.CostEstimate(
            flops=4 * count * length * tiles * pair, bytes_accessed=3 << 20, transcendentals=0
        ),
        name="convolve",
    )(turned, spectrum, table)


def project_kernel(place_ref, conv_ref, mixed_ref, query_ref, skip_ref, weight_ref, out_ref, gated):
    @pl.when(pl.program_id(0) == 0)
    def _():
        conv = conv_ref[...].T.astype(jnp.float32)
        combined = conv + skip_ref[...] * mixed_ref[...].astype(jnp.float32)
        gated[...] = (query_ref[...].astype(jnp.float32) * combined).astype(jnp.bfloat16)

    out_ref[0] = jnp.dot(gated[...], weight_ref[...], preferred_element_type=jnp.float32).astype(jnp.bfloat16)


def project(blocks, conv_turned, mixed, query_gate, skip_gain, out_weight):
    length, width = mixed.shape
    number = blocks.shape[0]
    return pl.pallas_call(
        project_kernel,
        grid_spec=pltpu.PrefetchScalarGridSpec(
            num_scalar_prefetch=1,
            grid=(number,),
            in_specs=[
                pl.BlockSpec((width, length), lambda i, blocks: (0, 0)),
                pl.BlockSpec((length, width), lambda i, blocks: (0, 0)),
                pl.BlockSpec((length, width), lambda i, blocks: (0, 0)),
                pl.BlockSpec((1, width), lambda i, blocks: (0, 0)),
                pl.BlockSpec((width, width), lambda i, blocks: (0, blocks[i])),
            ],
            out_specs=pl.BlockSpec((1, length, width), lambda i, blocks: (i, 0, 0)),
            scratch_shapes=[pltpu.VMEM((length, width), jnp.bfloat16)],
        ),
        out_shape=jax.ShapeDtypeStruct((number, length, width), jnp.bfloat16),
        cost_estimate=pl.CostEstimate(
            flops=2 * length * width * width * number, bytes_accessed=10 << 20, transcendentals=0
        ),
        name="project",
    )(blocks, conv_turned, mixed, query_gate, skip_gain.reshape(1, width), out_weight)


def added(*terms):
    total = terms[0].astype(jnp.float32)
    for term in terms[1:]:
        total = total + term.astype(jnp.float32)
    return total.astype(jnp.bfloat16)


def body(query_gate, key_gate, value_in, filter_taps, skip_gain, out_weight):
    length, width = query_gate.shape
    ctx, groups = lax.axis_size("ctx"), lax.axis_size("ch")
    ring = groups // CORES
    few = width // ctx
    here, group = lax.axis_index("ctx"), lax.axis_index("ch")
    y, core = group // CORES, group % CORES
    per_tile = LANES // few
    table = jnp.asarray(odd_tables(length))

    mixed, turned = mix(key_gate, value_in)
    place = jnp.stack([here // per_tile, here % per_tile]).astype(jnp.int32)
    spectrum = taps_spectrum(place, filter_taps, table, few)
    long_rows = lax.all_to_all(turned.reshape(ctx, few, length), "ctx", 0, 0)
    conv_rows = convolve(long_rows.reshape(ctx * few, length), spectrum, table, few)
    conv_turned = lax.all_to_all(conv_rows.reshape(ctx, few, length), "ctx", 0, 0).reshape(width, length)

    ahead = (y + jnp.array([2, 1, 3, 0], jnp.int32)) % ring
    blocks = jnp.concatenate([ahead * CORES + (1 - core), ahead * CORES + core]).astype(jnp.int32)
    parts = project(blocks, conv_turned, mixed, query_gate, skip_gain, out_weight)

    def ch_shift(block, dy, dcore):
        route = [(i, ((i // CORES + dy) % ring) * CORES + (i % CORES + dcore) % CORES) for i in range(groups)]
        return lax.ppermute(block, "ch", route)

    partner = ch_shift(parts[:ring], 0, 1)
    half = length // 2
    across_low = added(parts[ring, :half], partner[0, :half])
    across_high = added(parts[ring, half:], partner[0, half:])
    got_across_low = ch_shift(across_low, 1, 0)
    got_across_high = ch_shift(across_high, -1, 0)
    up_high = ch_shift(added(parts[ring + 1, half:], partner[1, half:]), 1, 0)
    down_low = ch_shift(added(parts[ring + 2, :half], partner[2, :half]), -1, 0)
    up_low = ch_shift(added(parts[ring + 1, :half], partner[1, :half], got_across_low), 1, 0)
    down_high = ch_shift(added(parts[ring + 2, half:], partner[2, half:], got_across_high), -1, 0)
    low = added(parts[ring + 3, :half], partner[3, :half], down_low, up_low)
    high = added(parts[ring + 3, half:], partner[3, half:], up_high, down_high)
    return jnp.concatenate([low, high], axis=0)


def solution(mesh):
    in_specs = (
        P("ctx", "ch"),
        P("ctx", "ch"),
        P("ctx", "ch"),
        P(None, "ch"),
        P("ch"),
        P("ch", None),
    )
    out_specs = P("ctx", "ch")
    return jax.shard_map(body, mesh=mesh, in_specs=in_specs, out_specs=out_specs, check_vma=False)
```

```python
import functools

import jax
import jax.numpy as jnp
import numpy as np
from jax import lax
from jax.experimental import pallas as pl
from jax.experimental.pallas import tpu as pltpu
from jax.sharding import PartitionSpec as P

WIN = 8
LANES = 128
CORES = 2
PARAMS = pltpu.CompilerParams(vmem_limit_bytes=20 << 20)


def odd_tables(length):
    order = np.concatenate([np.arange(0, length, 2), np.arange(1, length, 2)])
    turns = (np.arange(length)[:, None] * (2 * order[None, :] + 1)) % (4 * length)
    angle = turns * (np.pi / (2 * length))
    tiles = length // LANES
    cos_part = np.cos(angle).reshape(length, tiles, LANES)
    sin_part = -np.sin(angle).reshape(length, tiles, LANES)
    table = np.concatenate([cos_part, sin_part], axis=2).transpose(1, 0, 2)
    return table.astype(jnp.bfloat16)


def mix_kernel(key_ref, value_ref, mixed_ref, turned_ref):
    product = (key_ref[...].astype(jnp.float32) * value_ref[...].astype(jnp.float32)).astype(jnp.bfloat16)
    mixed_ref[...] = product
    turned_ref[...] = product.T


def mix(key_gate, value_in):
    length, width = key_gate.shape
    return pl.pallas_call(
        mix_kernel,
        grid=(width // LANES,),
        in_specs=[pl.BlockSpec((length, LANES), lambda i: (0, i))] * 2,
        out_specs=[
            pl.BlockSpec((length, LANES), lambda i: (0, i)),
            pl.BlockSpec((LANES, length), lambda i: (i, 0)),
        ],
        out_shape=[
            jax.ShapeDtypeStruct((length, width), jnp.bfloat16),
            jax.ShapeDtypeStruct((width, length), jnp.bfloat16),
        ],
        cost_estimate=pl.CostEstimate(flops=length * width, bytes_accessed=8 * length * width, transcendentals=0),
        name="mix",
    )(key_gate, value_in)


def taps_kernel(few, place_ref, taps_ref, table_ref, out_ref, turned):
    step = pl.program_id(0)
    length = table_ref.shape[1]
    first = place_ref[1] * few
    rows = lax.broadcasted_iota(jnp.int32, (few, LANES), 0)
    lanes = lax.broadcasted_iota(jnp.int32, (few, LANES), 1)
    pick = (lanes == rows + first).astype(jnp.bfloat16)
    picked = lax.dot_general(
        pick, taps_ref[...].astype(jnp.bfloat16), (((1,), (1,)), ((), ())), preferred_element_type=jnp.float32
    ).astype(jnp.bfloat16)
    for half in range(2):
        start = pl.multiple_of((2 * step + half) * few, few)
        turned[pl.ds(start, few), :] = picked[:, half * length : (half + 1) * length]

    @pl.when(step == pl.num_programs(0) - 1)
    def _():
        for tile in range(table_ref.shape[0]):
            out_ref[tile] = jnp.dot(turned[...], table_ref[tile], preferred_element_type=jnp.float32)


def taps_spectrum(place, filter_taps, table, few):
    tiles, length, pair = table.shape
    rows = WIN * few
    return pl.pallas_call(
        functools.partial(taps_kernel, few),
        grid_spec=pltpu.PrefetchScalarGridSpec(
            num_scalar_prefetch=1,
            grid=(WIN // 2,),
            in_specs=[
                pl.BlockSpec((2 * length, LANES), lambda i, place: (i, place[0])),
                pl.BlockSpec((tiles, length, pair), lambda i, place: (0, 0, 0)),
            ],
            out_specs=pl.BlockSpec((tiles, rows, pair), lambda i, place: (0, 0, 0)),
            scratch_shapes=[pltpu.VMEM((rows, length), jnp.bfloat16)],
        ),
        out_shape=jax.ShapeDtypeStruct((tiles, rows, pair), jnp.float32),
        cost_estimate=pl.CostEstimate(
            flops=2 * rows * length * tiles * pair, bytes_accessed=3 << 20, transcendentals=0
        ),
        name="taps_spectrum",
    )(place, filter_taps, table)


def conv_kernel(few, x_ref, h_ref, table_ref, out_ref, window, total, product, gathered):
    tile = pl.program_id(0)
    tiles = pl.num_programs(0)
    count, length = x_ref.shape
    spans = count // few
    spectrum = jnp.dot(x_ref[...], table_ref[0], preferred_element_type=jnp.float32)
    real, imag = spectrum[:, :LANES], spectrum[:, LANES:]
    sign = jnp.where(tile < tiles // 2, 1.0, -1.0).astype(jnp.float32)
    zero = jnp.zeros((few, LANES), jnp.float32)
    before_real = jnp.concatenate([zero, real[:-few]], axis=0)
    before_imag = jnp.concatenate([zero, imag[:-few]], axis=0)
    window_real = before_real + sign * imag
    window_imag = before_imag - sign * real
    window[0] = window_real
    window[1] = window_imag
    window[2] = window_real + window_imag
    for part in range(few // 8):
        low = part * 8
        first, plus, minus = [], [], []
        for lag in range(WIN):
            h_real = h_ref[0, lag * few + low : lag * few + low + 8, :LANES]
            h_imag = h_ref[0, lag * few + low : lag * few + low + 8, LANES:]
            first.append(h_real)
            plus.append(h_real + h_imag)
            minus.append(h_imag - h_real)
        for span in range(spans):
            one = two = three = None
            for lag in range(min(WIN, span + 1)):
                at = (span - lag) * few + low
                term_one = first[lag] * window[2, at : at + 8, :]
                term_two = plus[lag] * window[1, at : at + 8, :]
                term_three = minus[lag] * window[0, at : at + 8, :]
                one = term_one if one is None else one + term_one
                two = term_two if two is None else two + term_two
                three = term_three if three is None else three + term_three
            at = span * few + low
            total[0, at : at + 8, :] = one + three
            total[1, at : at + 8, :] = one - two
    scale = sign * (1.0 / length)
    product[:, :LANES] = (-scale * total[0]).astype(jnp.bfloat16)
    product[:, LANES:] = (scale * total[1]).astype(jnp.bfloat16)
    part_out = lax.dot_general(
        product[...], table_ref[0], (((1,), (1,)), ((), ())), preferred_element_type=jnp.float32
    )

    @pl.when(tile == 0)
    def _():
        gathered[...] = part_out

    @pl.when(tile > 0)
    def _():
        gathered[...] += part_out

    @pl.when(tile == tiles - 1)
    def _():
        out_ref[...] = gathered[...].astype(jnp.bfloat16)


def convolve(turned, spectrum, table, few):
    count, length = turned.shape
    tiles, _, pair = table.shape
    rows = WIN * few
    return pl.pallas_call(
        functools.partial(conv_kernel, few),
        grid=(tiles,),
        in_specs=[
            pl.BlockSpec((count, length), lambda i: (0, 0)),
            pl.BlockSpec((1, rows, pair), lambda i: (i, 0, 0)),
            pl.BlockSpec((1, length, pair), lambda i: (i, 0, 0)),
        ],
        out_specs=pl.BlockSpec((count, length), lambda i: (0, 0)),
        out_shape=jax.ShapeDtypeStruct((count, length), jnp.bfloat16),
        scratch_shapes=[
            pltpu.VMEM((3, count, LANES), jnp.float32),
            pltpu.VMEM((2, count, LANES), jnp.float32),
            pltpu.VMEM((count, pair), jnp.bfloat16),
            pltpu.VMEM((count, length), jnp.float32),
        ],
        cost_estimate=pl.CostEstimate(
            flops=4 * count * length * tiles * pair, bytes_accessed=3 << 20, transcendentals=0
        ),
        compiler_params=PARAMS,
        name="convolve",
    )(turned, spectrum, table)


def gate_kernel(conv_ref, mixed_ref, query_ref, skip_ref, gated_ref):
    conv = conv_ref[...].T.astype(jnp.float32)
    combined = conv + skip_ref[...] * mixed_ref[...].astype(jnp.float32)
    gated_ref[...] = (query_ref[...].astype(jnp.float32) * combined).astype(jnp.bfloat16)


def gate(conv_turned, mixed, query_gate, skip_gain):
    length, width = mixed.shape
    return pl.pallas_call(
        gate_kernel,
        out_shape=jax.ShapeDtypeStruct((length, width), jnp.bfloat16),
        compiler_params=PARAMS,
        cost_estimate=pl.CostEstimate(flops=4 * length * width, bytes_accessed=8 * length * width, transcendentals=0),
        name="gate",
    )(conv_turned, mixed, query_gate, skip_gain.reshape(1, width))


def weights_kernel(number, blocks_ref, weight_ref, own_ref, partner_ref, sems):
    width = weight_ref.shape[0]
    copies = []
    for k in range(number):
        for at, ref in enumerate((partner_ref, own_ref)):
            start = pl.multiple_of(blocks_ref[number * at + k] * width, width)
            copies.append(
                pltpu.make_async_copy(weight_ref.at[:, pl.ds(start, width)], ref.at[k], sems.at[number * at + k])
            )
    for copy in copies:
        copy.start()
    for copy in copies:
        copy.wait()


def weight_blocks(blocks, out_weight):
    width = out_weight.shape[0]
    number = blocks.shape[0] // 2
    shape = jax.ShapeDtypeStruct((number, width, width), jnp.bfloat16)
    return pl.pallas_call(
        functools.partial(weights_kernel, number),
        grid_spec=pltpu.PrefetchScalarGridSpec(
            num_scalar_prefetch=1,
            in_specs=[pl.BlockSpec(memory_space=pl.ANY)],
            out_specs=[pl.BlockSpec(memory_space=pltpu.VMEM)] * 2,
            scratch_shapes=[pltpu.SemaphoreType.DMA((2 * number,))],
        ),
        out_shape=[shape] * 2,
        compiler_params=pltpu.CompilerParams(vmem_limit_bytes=48 << 20),
        cost_estimate=pl.CostEstimate(flops=0, bytes_accessed=8 << 20, transcendentals=0),
        name="weight_blocks",
    )(blocks, out_weight)


def own_part_kernel(number, gated_ref, weight_ref, out_ref):
    for k in range(number):
        out_ref[k] = jnp.dot(gated_ref[...], weight_ref[k], preferred_element_type=jnp.float32)


def own_part(gated, own_weight):
    length, width = gated.shape
    number = own_weight.shape[0]
    return pl.pallas_call(
        functools.partial(own_part_kernel, number),
        in_specs=[pl.BlockSpec(memory_space=pltpu.VMEM)] * 2,
        out_specs=pl.BlockSpec(memory_space=pltpu.VMEM),
        out_shape=jax.ShapeDtypeStruct((number, length, width), jnp.float32),
        compiler_params=PARAMS,
        cost_estimate=pl.CostEstimate(
            flops=2 * length * width * width * number, bytes_accessed=2 << 20, transcendentals=0
        ),
        name="own_part",
    )(gated, own_weight)


def project_kernel(which, part_ref, other_ref, weight_ref, *outs):
    half = other_ref.shape[0] // 2
    for at, k in enumerate(which):
        total = part_ref[k] + jnp.dot(other_ref[...], weight_ref[k], preferred_element_type=jnp.float32)
        total = total.astype(jnp.bfloat16)
        outs[2 * at][...] = total[:half]
        outs[2 * at + 1][...] = total[half:]


def project(which, part, other, other_weight):
    _, length, width = part.shape
    number = len(which)
    return pl.pallas_call(
        functools.partial(project_kernel, which),
        in_specs=[pl.BlockSpec(memory_space=pltpu.VMEM)] * 3,
        out_specs=[pl.BlockSpec(memory_space=pltpu.VMEM)] * (2 * number),
        out_shape=[jax.ShapeDtypeStruct((length // 2, width), jnp.bfloat16)] * (2 * number),
        compiler_params=PARAMS,
        cost_estimate=pl.CostEstimate(
            flops=2 * length * width * width * number, bytes_accessed=number << 20, transcendentals=0
        ),
        name="project",
    )(part, other, other_weight)


def finish_kernel(*refs):
    out_ref = refs[-1]
    half = out_ref.shape[0] // 2
    for at in range(2):
        total = sum(ref[...].astype(jnp.float32) for ref in refs[3 * at : 3 * at + 3])
        out_ref[at * half : (at + 1) * half, :] = total.astype(jnp.bfloat16)


def finish(low, high):
    half, width = low[0].shape
    return pl.pallas_call(
        finish_kernel,
        out_shape=jax.ShapeDtypeStruct((2 * half, width), jnp.bfloat16),
        compiler_params=PARAMS,
        cost_estimate=pl.CostEstimate(flops=6 * half * width, bytes_accessed=16 * half * width, transcendentals=0),
        name="finish",
    )(*low, *high)


def added(one, two):
    return (one.astype(jnp.float32) + two.astype(jnp.float32)).astype(jnp.bfloat16)


def body(query_gate, key_gate, value_in, filter_taps, skip_gain, out_weight):
    length, width = query_gate.shape
    ctx, groups = lax.axis_size("ctx"), lax.axis_size("ch")
    ring = groups // CORES
    few = width // ctx
    here, group = lax.axis_index("ctx"), lax.axis_index("ch")
    y, core = group // CORES, group % CORES
    per_tile = LANES // few
    table = jnp.asarray(odd_tables(length))

    def ch_shift(block, dy, dcore):
        route = [(i, ((i // CORES + dy) % ring) * CORES + (i % CORES + dcore) % CORES) for i in range(groups)]
        return lax.ppermute(block, "ch", route)

    mixed, turned = mix(key_gate, value_in)
    place = jnp.stack([here // per_tile, here % per_tile]).astype(jnp.int32)
    spectrum = taps_spectrum(place, filter_taps, table, few)
    ahead = [(y + step) % ring for step in (2, 1, 3, 0)]
    blocks = jnp.stack([k * CORES + at for at in (1 - core, core) for k in ahead]).astype(jnp.int32)
    own_weight, partner_weight = weight_blocks(blocks, out_weight)
    other_weight = ch_shift(partner_weight, 0, 1)

    long_rows = lax.all_to_all(turned.reshape(ctx, few, length), "ctx", 0, 0)
    conv_rows = convolve(long_rows.reshape(ctx * few, length), spectrum, table, few)
    conv_turned = lax.all_to_all(conv_rows.reshape(ctx, few, length), "ctx", 0, 0).reshape(width, length)

    gated = gate(conv_turned, mixed, query_gate, skip_gain)
    other = ch_shift(gated, 0, 1)
    part = own_part(gated, own_weight)
    across_low, across_high = project((0,), part, other, other_weight)
    got_low = ch_shift(across_low, 1, 0)
    got_high = ch_shift(across_high, -1, 0)
    up_low, up_high, down_low, down_high, own_low, own_high = project((1, 2, 3), part, other, other_weight)
    from_below_high = ch_shift(up_high, 1, 0)
    from_above_low = ch_shift(down_low, -1, 0)
    from_below_low = ch_shift(added(up_low, got_low), 1, 0)
    from_above_high = ch_shift(added(down_high, got_high), -1, 0)
    return finish((own_low, from_above_low, from_below_low), (own_high, from_below_high, from_above_high))


def solution(mesh):
    in_specs = (
        P("ctx", "ch"),
        P("ctx", "ch"),
        P("ctx", "ch"),
        P(None, "ch"),
        P("ch"),
        P("ch", None),
    )
    out_specs = P("ctx", "ch")
    return jax.shard_map(body, mesh=mesh, in_specs=in_specs, out_specs=out_specs, check_vma=False)
```

```python
import functools

import jax
import jax.numpy as jnp
import numpy as np
from jax import lax
from jax.experimental import pallas as pl
from jax.experimental.pallas import tpu as pltpu
from jax.sharding import PartitionSpec as P

WIN = 8
LANES = 128
CORES = 2
PARAMS = pltpu.CompilerParams(vmem_limit_bytes=20 << 20)


def odd_tables(length):
    order = np.concatenate([np.arange(0, length, 2), np.arange(1, length, 2)])
    turns = (np.arange(length)[:, None] * (2 * order[None, :] + 1)) % (4 * length)
    angle = turns * (np.pi / (2 * length))
    tiles = length // LANES
    cos_part = np.cos(angle).reshape(length, tiles, LANES)
    sin_part = -np.sin(angle).reshape(length, tiles, LANES)
    table = np.concatenate([cos_part, sin_part], axis=2).transpose(1, 0, 2)
    return table.astype(jnp.bfloat16)


def mix_kernel(chunks, key_ref, value_ref, mixed_ref, turned_ref, keys, values, sems):
    size = key_ref.shape[0] // chunks

    def fetch(k):
        rows = pl.ds(k * size, size)
        return (
            pltpu.make_async_copy(key_ref.at[rows], keys.at[rows], sems.at[0, k]),
            pltpu.make_async_copy(value_ref.at[rows], values.at[rows], sems.at[1, k]),
        )

    for k in range(chunks):
        for copy in fetch(k):
            copy.start()
    for k in range(chunks):
        for copy in fetch(k):
            copy.wait()
        rows = slice(k * size, (k + 1) * size)
        product = (keys[rows, :].astype(jnp.float32) * values[rows, :].astype(jnp.float32)).astype(jnp.bfloat16)
        mixed_ref[rows, :] = product
        turned_ref[:, rows] = product.T


def mix(key_gate, value_in):
    length, width = key_gate.shape
    chunks = length // LANES
    return pl.pallas_call(
        functools.partial(mix_kernel, chunks),
        in_specs=[pl.BlockSpec(memory_space=pl.ANY)] * 2,
        out_specs=[pl.BlockSpec(memory_space=pltpu.VMEM)] * 2,
        out_shape=[
            jax.ShapeDtypeStruct((length, width), jnp.bfloat16),
            jax.ShapeDtypeStruct((width, length), jnp.bfloat16),
        ],
        scratch_shapes=[pltpu.VMEM((length, width), jnp.bfloat16)] * 2 + [pltpu.SemaphoreType.DMA((2, chunks))],
        cost_estimate=pl.CostEstimate(flops=length * width, bytes_accessed=8 * length * width, transcendentals=0),
        name="mix",
    )(key_gate, value_in)


def taps_kernel(few, place_ref, taps_ref, table_ref, out_ref, taps, turned, sems):
    tiles, length, _ = table_ref.shape
    column = pl.multiple_of(place_ref[0] * LANES, LANES)

    def fetch(k):
        rows = pl.ds(k * length, length)
        return pltpu.make_async_copy(taps_ref.at[rows, pl.ds(column, LANES)], taps.at[rows], sems.at[k])

    for k in range(WIN):
        fetch(k).start()
    first = place_ref[1] * few
    rows = lax.broadcasted_iota(jnp.int32, (few, LANES), 0)
    lanes = lax.broadcasted_iota(jnp.int32, (few, LANES), 1)
    pick = (lanes == rows + first).astype(jnp.bfloat16)
    for k in range(WIN):
        fetch(k).wait()
        picked = lax.dot_general(
            pick,
            taps[k * length : (k + 1) * length, :].astype(jnp.bfloat16),
            (((1,), (1,)), ((), ())),
            preferred_element_type=jnp.float32,
        )
        turned[k * few : (k + 1) * few, :] = picked.astype(jnp.bfloat16)
    for tile in range(tiles):
        out_ref[tile] = jnp.dot(turned[...], table_ref[tile], preferred_element_type=jnp.float32)


def taps_spectrum(place, filter_taps, table, few):
    tiles, length, pair = table.shape
    rows = WIN * few
    return pl.pallas_call(
        functools.partial(taps_kernel, few),
        grid_spec=pltpu.PrefetchScalarGridSpec(
            num_scalar_prefetch=1,
            in_specs=[pl.BlockSpec(memory_space=pl.ANY), pl.BlockSpec(memory_space=pltpu.VMEM)],
            out_specs=pl.BlockSpec(memory_space=pltpu.VMEM),
            scratch_shapes=[
                pltpu.VMEM((WIN * length, LANES), jnp.float32),
                pltpu.VMEM((rows, length), jnp.bfloat16),
                pltpu.SemaphoreType.DMA((WIN,)),
            ],
        ),
        out_shape=jax.ShapeDtypeStruct((tiles, rows, pair), jnp.float32),
        cost_estimate=pl.CostEstimate(
            flops=2 * rows * length * tiles * pair, bytes_accessed=3 << 20, transcendentals=0
        ),
        name="taps_spectrum",
    )(place, filter_taps, table)


def conv_kernel(few, x_ref, h_ref, table_ref, out_ref, rows, taps, table, window, product, sems):
    tiles, length, pair = table_ref.shape
    count = x_ref.shape[0]
    spans = count // few

    def fetch(k):
        if k == 0:
            return pltpu.make_async_copy(x_ref, rows, sems.at[0])
        tile = (k - 1) // 2
        if k % 2:
            return pltpu.make_async_copy(table_ref.at[tile], table.at[tile], sems.at[k])
        return pltpu.make_async_copy(h_ref.at[tile], taps.at[tile], sems.at[k])

    for k in range(1 + 2 * tiles):
        fetch(k).start()
    fetch(0).wait()
    for tile in range(tiles):
        fetch(1 + 2 * tile).wait()
        spectrum = jnp.dot(rows[...], table[tile], preferred_element_type=jnp.float32)
        fetch(2 + 2 * tile).wait()
        sign = 1.0 if tile < tiles // 2 else -1.0
        for span in range(spans):
            now = slice(span * few, (span + 1) * few)
            window_real = sign * spectrum[now, LANES:]
            window_imag = -sign * spectrum[now, :LANES]
            if span > 0:
                before = slice((span - 1) * few, span * few)
                window_real = spectrum[before, :LANES] + window_real
                window_imag = spectrum[before, LANES:] + window_imag
            window[tile, 0, now, :] = window_real
            window[tile, 1, now, :] = window_imag
            window[tile, 2, now, :] = window_real + window_imag
        first, plus, minus = [], [], []
        for lag in range(WIN):
            h_real = (-sign / length) * taps[tile, lag * few : (lag + 1) * few, :LANES]
            h_imag = (-sign / length) * taps[tile, lag * few : (lag + 1) * few, LANES:]
            first.append(h_real)
            plus.append(h_real + h_imag)
            minus.append(h_imag - h_real)
        for low in range(0, few, 8):
            part = slice(low, low + 8)
            for span in range(spans):
                one = two = three = None
                for lag in range(min(WIN, span + 1)):
                    at = (span - lag) * few + low
                    term_one = first[lag][part] * window[tile, 2, at : at + 8, :]
                    term_two = plus[lag][part] * window[tile, 1, at : at + 8, :]
                    term_three = minus[lag][part] * window[tile, 0, at : at + 8, :]
                    one = term_one if one is None else one + term_one
                    two = term_two if two is None else two + term_two
                    three = term_three if three is None else three + term_three
                at = span * few + low
                product[tile, at : at + 8, :LANES] = (one + three).astype(jnp.bfloat16)
                product[tile, at : at + 8, LANES:] = (two - one).astype(jnp.bfloat16)
    total = None
    for tile in range(tiles):
        term = lax.dot_general(
            product[tile], table[tile], (((1,), (1,)), ((), ())), preferred_element_type=jnp.float32
        )
        total = term if total is None else total + term
    out_ref[...] = total.astype(jnp.bfloat16)


def convolve(turned, spectrum, table, few):
    count, length = turned.shape
    tiles, _, pair = table.shape
    return pl.pallas_call(
        functools.partial(conv_kernel, few),
        in_specs=[pl.BlockSpec(memory_space=pl.ANY)] * 3,
        out_specs=pl.BlockSpec(memory_space=pltpu.VMEM),
        out_shape=jax.ShapeDtypeStruct((count, length), jnp.bfloat16),
        scratch_shapes=[
            pltpu.VMEM((count, length), jnp.bfloat16),
            pltpu.VMEM(spectrum.shape, jnp.float32),
            pltpu.VMEM(table.shape, jnp.bfloat16),
            pltpu.VMEM((tiles, 3, count, LANES), jnp.float32),
            pltpu.VMEM((tiles, count, pair), jnp.bfloat16),
            pltpu.SemaphoreType.DMA((1 + 2 * tiles,)),
        ],
        cost_estimate=pl.CostEstimate(
            flops=4 * count * length * tiles * pair, bytes_accessed=3 << 20, transcendentals=0
        ),
        name="convolve",
    )(turned, spectrum, table)


def gate_kernel(conv_ref, mixed_ref, query_ref, skip_ref, gated_ref):
    conv = conv_ref[...].T.astype(jnp.float32)
    combined = conv + skip_ref[...] * mixed_ref[...].astype(jnp.float32)
    gated_ref[...] = (query_ref[...].astype(jnp.float32) * combined).astype(jnp.bfloat16)


def gate(conv_turned, mixed, query_gate, skip_gain):
    length, width = mixed.shape
    return pl.pallas_call(
        gate_kernel,
        out_shape=jax.ShapeDtypeStruct((length, width), jnp.bfloat16),
        compiler_params=PARAMS,
        cost_estimate=pl.CostEstimate(flops=4 * length * width, bytes_accessed=8 * length * width, transcendentals=0),
        name="gate",
    )(conv_turned, mixed, query_gate, skip_gain.reshape(1, width))


def weights_kernel(number, blocks_ref, weight_ref, own_ref, partner_ref, sems):
    width = weight_ref.shape[0]
    copies = []
    for k in range(number):
        for at, ref in enumerate((partner_ref, own_ref)):
            start = pl.multiple_of(blocks_ref[number * at + k] * width, width)
            copies.append(
                pltpu.make_async_copy(weight_ref.at[:, pl.ds(start, width)], ref.at[k], sems.at[number * at + k])
            )
    for copy in copies:
        copy.start()
    for copy in copies:
        copy.wait()


def weight_blocks(blocks, out_weight):
    width = out_weight.shape[0]
    number = blocks.shape[0] // 2
    shape = jax.ShapeDtypeStruct((number, width, width), jnp.bfloat16)
    return pl.pallas_call(
        functools.partial(weights_kernel, number),
        grid_spec=pltpu.PrefetchScalarGridSpec(
            num_scalar_prefetch=1,
            in_specs=[pl.BlockSpec(memory_space=pl.ANY)],
            out_specs=[pl.BlockSpec(memory_space=pltpu.VMEM)] * 2,
            scratch_shapes=[pltpu.SemaphoreType.DMA((2 * number,))],
        ),
        out_shape=[shape] * 2,
        cost_estimate=pl.CostEstimate(flops=0, bytes_accessed=8 << 20, transcendentals=0),
        name="weight_blocks",
    )(blocks, out_weight)


def own_part_kernel(number, gated_ref, weight_ref, out_ref):
    for k in range(number):
        out_ref[k] = jnp.dot(gated_ref[...], weight_ref[k], preferred_element_type=jnp.float32)


def own_part(gated, own_weight):
    length, width = gated.shape
    number = own_weight.shape[0]
    return pl.pallas_call(
        functools.partial(own_part_kernel, number),
        in_specs=[pl.BlockSpec(memory_space=pltpu.VMEM)] * 2,
        out_specs=pl.BlockSpec(memory_space=pltpu.VMEM),
        out_shape=jax.ShapeDtypeStruct((number, length, width), jnp.float32),
        compiler_params=PARAMS,
        cost_estimate=pl.CostEstimate(
            flops=2 * length * width * width * number, bytes_accessed=2 << 20, transcendentals=0
        ),
        name="own_part",
    )(gated, own_weight)


def project_kernel(which, part_ref, other_ref, weight_ref, *outs):
    half = other_ref.shape[0] // 2
    for at, k in enumerate(which):
        total = part_ref[k] + jnp.dot(other_ref[...], weight_ref[k], preferred_element_type=jnp.float32)
        total = total.astype(jnp.bfloat16)
        outs[2 * at][...] = total[:half]
        outs[2 * at + 1][...] = total[half:]


def project(which, part, other, other_weight):
    _, length, width = part.shape
    number = len(which)
    return pl.pallas_call(
        functools.partial(project_kernel, which),
        in_specs=[pl.BlockSpec(memory_space=pltpu.VMEM)] * 3,
        out_specs=[pl.BlockSpec(memory_space=pltpu.VMEM)] * (2 * number),
        out_shape=[jax.ShapeDtypeStruct((length // 2, width), jnp.bfloat16)] * (2 * number),
        compiler_params=PARAMS,
        cost_estimate=pl.CostEstimate(
            flops=2 * length * width * width * number, bytes_accessed=number << 20, transcendentals=0
        ),
        name="project",
    )(part, other, other_weight)


def finish_kernel(*refs):
    out_ref = refs[-1]
    half = out_ref.shape[0] // 2
    for at in range(2):
        total = sum(ref[...].astype(jnp.float32) for ref in refs[3 * at : 3 * at + 3])
        out_ref[at * half : (at + 1) * half, :] = total.astype(jnp.bfloat16)


def finish(low, high):
    half, width = low[0].shape
    return pl.pallas_call(
        finish_kernel,
        out_shape=jax.ShapeDtypeStruct((2 * half, width), jnp.bfloat16),
        compiler_params=PARAMS,
        cost_estimate=pl.CostEstimate(flops=6 * half * width, bytes_accessed=16 * half * width, transcendentals=0),
        name="finish",
    )(*low, *high)


def added(one, two):
    return (one.astype(jnp.float32) + two.astype(jnp.float32)).astype(jnp.bfloat16)


def body(query_gate, key_gate, value_in, filter_taps, skip_gain, out_weight):
    length, width = query_gate.shape
    ctx, groups = lax.axis_size("ctx"), lax.axis_size("ch")
    ring = groups // CORES
    few = width // ctx
    here, group = lax.axis_index("ctx"), lax.axis_index("ch")
    y, core = group // CORES, group % CORES
    per_tile = LANES // few
    table = jnp.asarray(odd_tables(length))

    def ch_shift(block, dy, dcore):
        route = [(i, ((i // CORES + dy) % ring) * CORES + (i % CORES + dcore) % CORES) for i in range(groups)]
        return lax.ppermute(block, "ch", route)

    mixed, turned = mix(key_gate, value_in)
    place = jnp.stack([here // per_tile, here % per_tile]).astype(jnp.int32)
    spectrum = taps_spectrum(place, filter_taps, table, few)
    ahead = [(y + step) % ring for step in (2, 1, 3, 0)]
    blocks = jnp.stack([k * CORES + at for at in (1 - core, core) for k in ahead]).astype(jnp.int32)
    own_weight, partner_weight = weight_blocks(blocks, out_weight)
    other_weight = ch_shift(partner_weight, 0, 1)

    long_rows = lax.all_to_all(turned.reshape(ctx, few, length), "ctx", 0, 0)
    conv_rows = convolve(long_rows.reshape(ctx * few, length), spectrum, table, few)
    conv_turned = lax.all_to_all(conv_rows.reshape(ctx, few, length), "ctx", 0, 0).reshape(width, length)

    gated = gate(conv_turned, mixed, query_gate, skip_gain)
    other = ch_shift(gated, 0, 1)
    part = own_part(gated, own_weight)
    across_low, across_high = project((0,), part, other, other_weight)
    got_low = ch_shift(across_low, 1, 0)
    got_high = ch_shift(across_high, -1, 0)
    up_low, up_high, down_low, down_high, own_low, own_high = project((1, 2, 3), part, other, other_weight)
    from_below_high = ch_shift(up_high, 1, 0)
    from_above_low = ch_shift(down_low, -1, 0)
    from_below_low = ch_shift(added(up_low, got_low), 1, 0)
    from_above_high = ch_shift(added(down_high, got_high), -1, 0)
    return finish((own_low, from_above_low, from_below_low), (own_high, from_below_high, from_above_high))


def solution(mesh):
    in_specs = (
        P("ctx", "ch"),
        P("ctx", "ch"),
        P("ctx", "ch"),
        P(None, "ch"),
        P("ch"),
        P("ch", None),
    )
    out_specs = P("ctx", "ch")
    return jax.shard_map(body, mesh=mesh, in_specs=in_specs, out_specs=out_specs, check_vma=False)
```

```python
import functools

import jax
import jax.numpy as jnp
import numpy as np
from jax import lax
from jax.experimental import pallas as pl
from jax.experimental.pallas import tpu as pltpu
from jax.sharding import PartitionSpec as P

WIN = 8
LANES = 128
CORES = 2
CHUNKS = 2
PARAMS = pltpu.CompilerParams(vmem_limit_bytes=20 << 20)


def odd_tables(length):
    order = np.concatenate([np.arange(0, length, 2), np.arange(1, length, 2)])
    turns = (np.arange(length)[:, None] * (2 * order[None, :] + 1)) % (4 * length)
    angle = turns * (np.pi / (2 * length))
    tiles = length // LANES
    cos_part = np.cos(angle).reshape(length, tiles, LANES)
    sin_part = -np.sin(angle).reshape(length, tiles, LANES)
    table = np.concatenate([cos_part, sin_part], axis=2).transpose(1, 0, 2)
    return table.astype(jnp.bfloat16)


def mixed_of(key, value):
    return (key.astype(jnp.float32) * value.astype(jnp.float32)).astype(jnp.bfloat16)


def mix_kernel(chunks, key_ref, value_ref, turned_ref, keys, values, turned, sems):
    size = key_ref.shape[0] // chunks
    share = turned_ref.shape[0] // chunks

    def fetch(k):
        rows = pl.ds(k * size, size)
        return (
            pltpu.make_async_copy(key_ref.at[rows], keys.at[rows], sems.at[0, k]),
            pltpu.make_async_copy(value_ref.at[rows], values.at[rows], sems.at[1, k]),
        )

    def put(k):
        rows = pl.ds(k * share, share)
        return pltpu.make_async_copy(turned.at[rows], turned_ref.at[rows], sems.at[2, k])

    for k in range(chunks):
        for copy in fetch(k):
            copy.start()
    for k in range(chunks):
        for copy in fetch(k):
            copy.wait()
        rows = slice(k * size, (k + 1) * size)
        last = k == chunks - 1
        for at in range(chunks):
            columns = slice(at * share, (at + 1) * share)
            turned[columns, rows] = mixed_of(keys[rows, columns], values[rows, columns]).T
            if last:
                put(at).start()
    for k in range(chunks):
        put(k).wait()


def mix(key_gate, value_in):
    length, width = key_gate.shape
    chunks = length // LANES
    return pl.pallas_call(
        functools.partial(mix_kernel, chunks),
        in_specs=[pl.BlockSpec(memory_space=pl.ANY)] * 2,
        out_specs=pl.BlockSpec(memory_space=pl.ANY),
        out_shape=jax.ShapeDtypeStruct((width, length), jnp.bfloat16),
        scratch_shapes=[
            pltpu.VMEM((length, width), jnp.bfloat16),
            pltpu.VMEM((length, width), jnp.bfloat16),
            pltpu.VMEM((width, length), jnp.bfloat16),
            pltpu.SemaphoreType.DMA((3, chunks)),
        ],
        cost_estimate=pl.CostEstimate(flops=length * width, bytes_accessed=6 * length * width, transcendentals=0),
        name="mix",
    )(key_gate, value_in)


def taps_kernel(few, place_ref, taps_ref, table_ref, out_ref, taps, turned, sems):
    tiles, length, _ = table_ref.shape
    column = pl.multiple_of(place_ref[0] * LANES, LANES)

    def fetch(k):
        rows = pl.ds(k * length, length)
        return pltpu.make_async_copy(taps_ref.at[rows, pl.ds(column, LANES)], taps.at[rows], sems.at[k])

    for k in range(WIN):
        fetch(k).start()
    first = place_ref[1] * few
    rows = lax.broadcasted_iota(jnp.int32, (few, LANES), 0)
    lanes = lax.broadcasted_iota(jnp.int32, (few, LANES), 1)
    pick = (lanes == rows + first).astype(jnp.bfloat16)
    for k in range(WIN):
        fetch(k).wait()
        picked = lax.dot_general(
            pick,
            taps[k * length : (k + 1) * length, :].astype(jnp.bfloat16),
            (((1,), (1,)), ((), ())),
            preferred_element_type=jnp.float32,
        )
        turned[k * few : (k + 1) * few, :] = picked.astype(jnp.bfloat16)
    for tile in range(tiles):
        out_ref[tile] = jnp.dot(turned[...], table_ref[tile], preferred_element_type=jnp.float32)


def taps_spectrum(place, filter_taps, table, few):
    tiles, length, pair = table.shape
    rows = WIN * few
    return pl.pallas_call(
        functools.partial(taps_kernel, few),
        grid_spec=pltpu.PrefetchScalarGridSpec(
            num_scalar_prefetch=1,
            in_specs=[pl.BlockSpec(memory_space=pl.ANY), pl.BlockSpec(memory_space=pltpu.VMEM)],
            out_specs=pl.BlockSpec(memory_space=pltpu.VMEM),
            scratch_shapes=[
                pltpu.VMEM((WIN * length, LANES), jnp.float32),
                pltpu.VMEM((rows, length), jnp.bfloat16),
                pltpu.SemaphoreType.DMA((WIN,)),
            ],
        ),
        out_shape=jax.ShapeDtypeStruct((tiles, rows, pair), jnp.float32),
        cost_estimate=pl.CostEstimate(
            flops=2 * rows * length * tiles * pair, bytes_accessed=3 << 20, transcendentals=0
        ),
        name="taps_spectrum",
    )(place, filter_taps, table)


def conv_kernel(few, x_ref, h_ref, table_ref, out_ref, rows, taps, table, window, product, out, sems):
    tiles, length, pair = table_ref.shape
    count = x_ref.shape[0]
    spans = count // few

    size = count // CHUNKS

    def fetch(k):
        part = pl.ds(k * size, size)
        return pltpu.make_async_copy(x_ref.at[part], rows.at[part], sems.at[0, k])

    def fetch_table(tile):
        return pltpu.make_async_copy(table_ref.at[tile], table.at[tile], sems.at[1, tile])

    def fetch_taps(tile):
        return pltpu.make_async_copy(h_ref.at[tile], taps.at[tile], sems.at[2, tile])

    def put(k):
        part = pl.ds(k * size, size)
        return pltpu.make_async_copy(out.at[part], out_ref.at[part], sems.at[3, k])

    fetch_table(0).start()
    for k in range(CHUNKS):
        fetch(k).start()
    fetch_taps(0).start()
    for tile in range(1, tiles):
        fetch_table(tile).start()
        fetch_taps(tile).start()
    for tile in range(tiles):
        fetch_table(tile).wait()
        spectra = []
        for k in range(CHUNKS):
            if tile == 0:
                fetch(k).wait()
            spectra.append(
                jnp.dot(rows[k * size : (k + 1) * size, :], table[tile], preferred_element_type=jnp.float32)
            )
        spectrum = jnp.concatenate(spectra, axis=0)
        fetch_taps(tile).wait()
        sign = 1.0 if tile < tiles // 2 else -1.0
        for span in range(spans):
            now = slice(span * few, (span + 1) * few)
            window_real = sign * spectrum[now, LANES:]
            window_imag = -sign * spectrum[now, :LANES]
            if span > 0:
                before = slice((span - 1) * few, span * few)
                window_real = spectrum[before, :LANES] + window_real
                window_imag = spectrum[before, LANES:] + window_imag
            window[tile, 0, now, :] = window_real
            window[tile, 1, now, :] = window_imag
            window[tile, 2, now, :] = window_real + window_imag
        first, plus, minus = [], [], []
        for lag in range(WIN):
            h_real = (-sign / length) * taps[tile, lag * few : (lag + 1) * few, :LANES]
            h_imag = (-sign / length) * taps[tile, lag * few : (lag + 1) * few, LANES:]
            first.append(h_real)
            plus.append(h_real + h_imag)
            minus.append(h_imag - h_real)
        for low in range(0, few, 8):
            part = slice(low, low + 8)
            for span in range(spans):
                one = two = three = None
                for lag in range(min(WIN, span + 1)):
                    at = (span - lag) * few + low
                    term_one = first[lag][part] * window[tile, 2, at : at + 8, :]
                    term_two = plus[lag][part] * window[tile, 1, at : at + 8, :]
                    term_three = minus[lag][part] * window[tile, 0, at : at + 8, :]
                    one = term_one if one is None else one + term_one
                    two = term_two if two is None else two + term_two
                    three = term_three if three is None else three + term_three
                at = span * few + low
                product[tile, at : at + 8, :LANES] = (one + three).astype(jnp.bfloat16)
                product[tile, at : at + 8, LANES:] = (two - one).astype(jnp.bfloat16)
    for k in range(CHUNKS):
        part = slice(k * size, (k + 1) * size)
        total = None
        for tile in range(tiles):
            term = lax.dot_general(
                product[tile, part, :], table[tile], (((1,), (1,)), ((), ())), preferred_element_type=jnp.float32
            )
            total = term if total is None else total + term
        out[part, :] = total.astype(jnp.bfloat16)
        put(k).start()
    for k in range(CHUNKS):
        put(k).wait()


def convolve(turned, spectrum, table, few):
    count, length = turned.shape
    tiles, _, pair = table.shape
    return pl.pallas_call(
        functools.partial(conv_kernel, few),
        in_specs=[pl.BlockSpec(memory_space=pl.ANY)] * 3,
        out_specs=pl.BlockSpec(memory_space=pl.ANY),
        out_shape=jax.ShapeDtypeStruct((count, length), jnp.bfloat16),
        scratch_shapes=[
            pltpu.VMEM((count, length), jnp.bfloat16),
            pltpu.VMEM(spectrum.shape, jnp.float32),
            pltpu.VMEM(table.shape, jnp.bfloat16),
            pltpu.VMEM((tiles, 3, count, LANES), jnp.float32),
            pltpu.VMEM((tiles, count, pair), jnp.bfloat16),
            pltpu.VMEM((count, length), jnp.bfloat16),
            pltpu.SemaphoreType.DMA((4, tiles)),
        ],
        cost_estimate=pl.CostEstimate(
            flops=4 * count * length * tiles * pair, bytes_accessed=3 << 20, transcendentals=0
        ),
        name="convolve",
    )(turned, spectrum, table)


def gate_kernel(conv_ref, mixed_ref, query_ref, skip_ref, gated_ref):
    conv = conv_ref[...].T.astype(jnp.float32)
    combined = conv + skip_ref[...] * mixed_ref[...].astype(jnp.float32)
    gated_ref[...] = (query_ref[...].astype(jnp.float32) * combined).astype(jnp.bfloat16)


def gate(conv_turned, mixed, query_gate, skip_gain):
    length, width = query_gate.shape
    return pl.pallas_call(
        gate_kernel,
        out_shape=jax.ShapeDtypeStruct((length, width), jnp.bfloat16),
        compiler_params=PARAMS,
        cost_estimate=pl.CostEstimate(flops=4 * length * width, bytes_accessed=8 * length * width, transcendentals=0),
        name="gate",
    )(conv_turned, mixed, query_gate, skip_gain.reshape(1, width))


def weights_kernel(number, blocks_ref, weight_ref, own_ref, partner_ref, sems):
    width = weight_ref.shape[0]
    copies = []
    for k in range(number):
        for at, ref in enumerate((partner_ref, own_ref)):
            start = pl.multiple_of(blocks_ref[number * at + k] * width, width)
            copies.append(
                pltpu.make_async_copy(weight_ref.at[:, pl.ds(start, width)], ref.at[k], sems.at[number * at + k])
            )
    for copy in copies:
        copy.start()
    for copy in copies:
        copy.wait()


def weight_blocks(blocks, out_weight):
    width = out_weight.shape[0]
    number = blocks.shape[0] // 2
    shape = jax.ShapeDtypeStruct((number, width, width), jnp.bfloat16)
    return pl.pallas_call(
        functools.partial(weights_kernel, number),
        grid_spec=pltpu.PrefetchScalarGridSpec(
            num_scalar_prefetch=1,
            in_specs=[pl.BlockSpec(memory_space=pl.ANY)],
            out_specs=[pl.BlockSpec(memory_space=pltpu.VMEM)] * 2,
            scratch_shapes=[pltpu.SemaphoreType.DMA((2 * number,))],
        ),
        out_shape=[shape] * 2,
        cost_estimate=pl.CostEstimate(flops=0, bytes_accessed=8 << 20, transcendentals=0),
        name="weight_blocks",
    )(blocks, out_weight)


def own_part_kernel(number, gated_ref, weight_ref, out_ref):
    for k in range(number):
        out_ref[k] = jnp.dot(gated_ref[...], weight_ref[k], preferred_element_type=jnp.float32)


def own_part(gated, own_weight):
    length, width = gated.shape
    number = own_weight.shape[0]
    return pl.pallas_call(
        functools.partial(own_part_kernel, number),
        in_specs=[pl.BlockSpec(memory_space=pltpu.VMEM)] * 2,
        out_specs=pl.BlockSpec(memory_space=pltpu.VMEM),
        out_shape=jax.ShapeDtypeStruct((number, length, width), jnp.float32),
        compiler_params=PARAMS,
        cost_estimate=pl.CostEstimate(
            flops=2 * length * width * width * number, bytes_accessed=2 << 20, transcendentals=0
        ),
        name="own_part",
    )(gated, own_weight)


def project_kernel(which, part_ref, other_ref, weight_ref, *outs):
    half = other_ref.shape[0] // 2
    for at, k in enumerate(which):
        total = part_ref[k] + jnp.dot(other_ref[...], weight_ref[k], preferred_element_type=jnp.float32)
        total = total.astype(jnp.bfloat16)
        outs[2 * at][...] = total[:half]
        outs[2 * at + 1][...] = total[half:]


def project(which, part, other, other_weight):
    _, length, width = part.shape
    number = len(which)
    return pl.pallas_call(
        functools.partial(project_kernel, which),
        in_specs=[pl.BlockSpec(memory_space=pltpu.VMEM)] * 3,
        out_specs=[pl.BlockSpec(memory_space=pltpu.VMEM)] * (2 * number),
        out_shape=[jax.ShapeDtypeStruct((length // 2, width), jnp.bfloat16)] * (2 * number),
        compiler_params=PARAMS,
        cost_estimate=pl.CostEstimate(
            flops=2 * length * width * width * number, bytes_accessed=number << 20, transcendentals=0
        ),
        name="project",
    )(part, other, other_weight)


def finish_kernel(*refs):
    out_ref, out, sems = refs[6:]
    half = refs[0].shape[0]
    size = half // 2

    def put(k):
        part = pl.ds(k * size, size)
        return pltpu.make_async_copy(out.at[part], out_ref.at[part], sems.at[k])

    for k in range(4):
        rows = slice(k % 2 * size, (k % 2 + 1) * size)
        total = sum(ref[rows, :].astype(jnp.float32) for ref in refs[3 * (k // 2) : 3 * (k // 2) + 3])
        out[k * size : (k + 1) * size, :] = total.astype(jnp.bfloat16)
        put(k).start()
    for k in range(4):
        put(k).wait()


def finish(low, high):
    half, width = low[0].shape
    return pl.pallas_call(
        finish_kernel,
        in_specs=[pl.BlockSpec(memory_space=pltpu.VMEM)] * 6,
        out_specs=pl.BlockSpec(memory_space=pl.ANY),
        out_shape=jax.ShapeDtypeStruct((2 * half, width), jnp.bfloat16),
        scratch_shapes=[pltpu.VMEM((2 * half, width), jnp.bfloat16), pltpu.SemaphoreType.DMA((4,))],
        compiler_params=PARAMS,
        cost_estimate=pl.CostEstimate(flops=6 * half * width, bytes_accessed=16 * half * width, transcendentals=0),
        name="finish",
    )(*low, *high)


def added(one, two):
    return (one.astype(jnp.float32) + two.astype(jnp.float32)).astype(jnp.bfloat16)


def body(query_gate, key_gate, value_in, filter_taps, skip_gain, out_weight):
    length, width = query_gate.shape
    ctx, groups = lax.axis_size("ctx"), lax.axis_size("ch")
    ring = groups // CORES
    few = width // ctx
    here, group = lax.axis_index("ctx"), lax.axis_index("ch")
    y, core = group // CORES, group % CORES
    per_tile = LANES // few
    table = jnp.asarray(odd_tables(length))

    def ch_shift(block, dy, dcore):
        route = [(i, ((i // CORES + dy) % ring) * CORES + (i % CORES + dcore) % CORES) for i in range(groups)]
        return lax.ppermute(block, "ch", route)

    turned = mix(key_gate, value_in)
    place = jnp.stack([here // per_tile, here % per_tile]).astype(jnp.int32)
    spectrum = taps_spectrum(place, filter_taps, table, few)
    ahead = [(y + step) % ring for step in (2, 1, 3, 0)]
    blocks = jnp.stack([k * CORES + at for at in (1 - core, core) for k in ahead]).astype(jnp.int32)
    own_weight, partner_weight = weight_blocks(blocks, out_weight)
    other_weight = ch_shift(partner_weight, 0, 1)

    long_rows = lax.all_to_all(turned.reshape(ctx, few, length), "ctx", 0, 0)
    conv_rows = convolve(long_rows.reshape(ctx * few, length), spectrum, table, few)
    conv_turned = lax.all_to_all(conv_rows.reshape(ctx, few, length), "ctx", 0, 0).reshape(width, length)

    gated = gate(conv_turned, mixed_of(key_gate, value_in), query_gate, skip_gain)
    other = ch_shift(gated, 0, 1)
    part = own_part(gated, own_weight)
    across_low, across_high = project((0,), part, other, other_weight)
    got_low = ch_shift(across_low, 1, 0)
    got_high = ch_shift(across_high, -1, 0)
    up_low, up_high, down_low, down_high, own_low, own_high = project((1, 2, 3), part, other, other_weight)
    from_below_high = ch_shift(up_high, 1, 0)
    from_above_low = ch_shift(down_low, -1, 0)
    from_below_low = ch_shift(added(up_low, got_low), 1, 0)
    from_above_high = ch_shift(added(down_high, got_high), -1, 0)
    return finish((own_low, from_above_low, from_below_low), (own_high, from_below_high, from_above_high))


def solution(mesh):
    in_specs = (
        P("ctx", "ch"),
        P("ctx", "ch"),
        P("ctx", "ch"),
        P(None, "ch"),
        P("ch"),
        P("ch", None),
    )
    out_specs = P("ctx", "ch")
    return jax.shard_map(body, mesh=mesh, in_specs=in_specs, out_specs=out_specs, check_vma=False)
```

```python
import functools

import jax
import jax.numpy as jnp
import numpy as np
from jax import lax
from jax.experimental import pallas as pl
from jax.experimental.pallas import tpu as pltpu
from jax.sharding import PartitionSpec as P

WIN = 8
LANES = 128
CORES = 2
CONV_BYTES = 53 << 20
PARAMS = pltpu.CompilerParams(vmem_limit_bytes=20 << 20)


def odd_tables(length):
    order = np.concatenate([np.arange(0, length, 2), np.arange(1, length, 2)])
    turns = (np.arange(length)[:, None] * (2 * order[None, :] + 1)) % (4 * length)
    angle = turns * (np.pi / (2 * length))
    tiles = length // LANES
    cos_part = np.cos(angle).reshape(length, tiles, LANES)
    sin_part = -np.sin(angle).reshape(length, tiles, LANES)
    table = np.concatenate([cos_part, sin_part], axis=2).transpose(1, 0, 2)
    return table.astype(jnp.bfloat16)


def mix_kernel(chunks, key_ref, value_ref, mixed_ref, turned_ref, keys, values, sems):
    size = key_ref.shape[0] // chunks

    def fetch(k):
        rows = pl.ds(k * size, size)
        return (
            pltpu.make_async_copy(key_ref.at[rows], keys.at[rows], sems.at[0, k]),
            pltpu.make_async_copy(value_ref.at[rows], values.at[rows], sems.at[1, k]),
        )

    for k in range(chunks):
        for copy in fetch(k):
            copy.start()
    for k in range(chunks):
        for copy in fetch(k):
            copy.wait()
        rows = slice(k * size, (k + 1) * size)
        product = (keys[rows, :].astype(jnp.float32) * values[rows, :].astype(jnp.float32)).astype(jnp.bfloat16)
        mixed_ref[rows, :] = product
        turned_ref[:, rows] = product.T


def mix(key_gate, value_in):
    length, width = key_gate.shape
    chunks = length // LANES
    return pl.pallas_call(
        functools.partial(mix_kernel, chunks),
        in_specs=[pl.BlockSpec(memory_space=pl.ANY)] * 2,
        out_specs=[pl.BlockSpec(memory_space=pltpu.VMEM)] * 2,
        out_shape=[
            jax.ShapeDtypeStruct((length, width), jnp.bfloat16),
            jax.ShapeDtypeStruct((width, length), jnp.bfloat16),
        ],
        scratch_shapes=[pltpu.VMEM((length, width), jnp.bfloat16)] * 2 + [pltpu.SemaphoreType.DMA((2, chunks))],
        cost_estimate=pl.CostEstimate(flops=length * width, bytes_accessed=8 * length * width, transcendentals=0),
        name="mix",
    )(key_gate, value_in)


def taps_kernel(few, place_ref, taps_ref, table_ref, out_ref, taps, turned, sems):
    tiles, length, _ = table_ref.shape
    column = pl.multiple_of(place_ref[0] * LANES, LANES)

    def fetch(k):
        rows = pl.ds(k * length, length)
        return pltpu.make_async_copy(taps_ref.at[rows, pl.ds(column, LANES)], taps.at[rows], sems.at[k])

    for k in range(WIN):
        fetch(k).start()
    first = place_ref[1] * few
    rows = lax.broadcasted_iota(jnp.int32, (few, LANES), 0)
    lanes = lax.broadcasted_iota(jnp.int32, (few, LANES), 1)
    pick = (lanes == rows + first).astype(jnp.bfloat16)
    for k in range(WIN):
        fetch(k).wait()
        picked = lax.dot_general(
            pick,
            taps[k * length : (k + 1) * length, :].astype(jnp.bfloat16),
            (((1,), (1,)), ((), ())),
            preferred_element_type=jnp.float32,
        )
        turned[k * few : (k + 1) * few, :] = picked.astype(jnp.bfloat16)
    for tile in range(tiles):
        out_ref[tile] = jnp.dot(turned[...], table_ref[tile], preferred_element_type=jnp.float32)


def taps_spectrum(place, filter_taps, table, few):
    tiles, length, pair = table.shape
    rows = WIN * few
    return pl.pallas_call(
        functools.partial(taps_kernel, few),
        grid_spec=pltpu.PrefetchScalarGridSpec(
            num_scalar_prefetch=1,
            in_specs=[pl.BlockSpec(memory_space=pl.ANY), pl.BlockSpec(memory_space=pltpu.VMEM)],
            out_specs=pl.BlockSpec(memory_space=pltpu.VMEM),
            scratch_shapes=[
                pltpu.VMEM((WIN * length, LANES), jnp.float32),
                pltpu.VMEM((rows, length), jnp.bfloat16),
                pltpu.SemaphoreType.DMA((WIN,)),
            ],
        ),
        out_shape=jax.ShapeDtypeStruct((tiles, rows, pair), jnp.float32),
        cost_estimate=pl.CostEstimate(
            flops=2 * rows * length * tiles * pair, bytes_accessed=3 << 20, transcendentals=0
        ),
        name="taps_spectrum",
    )(place, filter_taps, table)


def conv_kernel(few, x_ref, h_ref, table_ref, out_ref, rows, taps, table, window, product, sems):
    tiles, length, pair = table_ref.shape
    count = x_ref.shape[0]
    spans = count // few

    def fetch_rows():
        return pltpu.make_async_copy(x_ref, rows, sems.at[0, 0])

    def fetch_table(tile):
        return pltpu.make_async_copy(table_ref.at[tile], table.at[tile], sems.at[1, tile])

    def fetch_taps(tile):
        return pltpu.make_async_copy(h_ref.at[tile], taps.at[tile], sems.at[2, tile])

    fetch_rows().start()
    fetch_table(0).start()
    fetch_taps(0).start()
    fetch_rows().wait()
    for tile in range(1, tiles):
        fetch_table(tile).start()
        fetch_taps(tile).start()
    for tile in range(tiles):
        fetch_table(tile).wait()
        spectrum = jnp.dot(rows[...], table[tile], preferred_element_type=jnp.float32)
        fetch_taps(tile).wait()
        sign = 1.0 if tile < tiles // 2 else -1.0
        for span in range(spans):
            now = slice(span * few, (span + 1) * few)
            window_real = sign * spectrum[now, LANES:]
            window_imag = -sign * spectrum[now, :LANES]
            if span > 0:
                before = slice((span - 1) * few, span * few)
                window_real = spectrum[before, :LANES] + window_real
                window_imag = spectrum[before, LANES:] + window_imag
            window[tile, 0, now, :] = window_real
            window[tile, 1, now, :] = window_imag
            window[tile, 2, now, :] = window_real + window_imag
        first, plus, minus = [], [], []
        for lag in range(WIN):
            h_real = (-sign / length) * taps[tile, lag * few : (lag + 1) * few, :LANES]
            h_imag = (-sign / length) * taps[tile, lag * few : (lag + 1) * few, LANES:]
            first.append(h_real)
            plus.append(h_real + h_imag)
            minus.append(h_imag - h_real)
        for low in range(0, few, 8):
            part = slice(low, low + 8)
            for span in range(spans):
                one = two = three = None
                for lag in range(min(WIN, span + 1)):
                    at = (span - lag) * few + low
                    term_one = first[lag][part] * window[tile, 2, at : at + 8, :]
                    term_two = plus[lag][part] * window[tile, 1, at : at + 8, :]
                    term_three = minus[lag][part] * window[tile, 0, at : at + 8, :]
                    one = term_one if one is None else one + term_one
                    two = term_two if two is None else two + term_two
                    three = term_three if three is None else three + term_three
                at = span * few + low
                product[tile, at : at + 8, :LANES] = (one + three).astype(jnp.bfloat16)
                product[tile, at : at + 8, LANES:] = (two - one).astype(jnp.bfloat16)
    total = None
    for tile in range(tiles):
        term = lax.dot_general(
            product[tile], table[tile], (((1,), (1,)), ((), ())), preferred_element_type=jnp.float32
        )
        total = term if total is None else total + term
    out_ref[...] = total.astype(jnp.bfloat16)


def convolve(turned, spectrum, table, few):
    count, length = turned.shape
    tiles, _, pair = table.shape
    return pl.pallas_call(
        functools.partial(conv_kernel, few),
        in_specs=[pl.BlockSpec(memory_space=pl.ANY)] * 3,
        out_specs=pl.BlockSpec(memory_space=pltpu.VMEM),
        out_shape=jax.ShapeDtypeStruct((count, length), jnp.bfloat16),
        scratch_shapes=[
            pltpu.VMEM((count, length), jnp.bfloat16),
            pltpu.VMEM(spectrum.shape, jnp.float32),
            pltpu.VMEM(table.shape, jnp.bfloat16),
            pltpu.VMEM((tiles, 3, count, LANES), jnp.float32),
            pltpu.VMEM((tiles, count, pair), jnp.bfloat16),
            pltpu.SemaphoreType.DMA((3, tiles)),
        ],
        compiler_params=pltpu.CompilerParams(vmem_limit_bytes=CONV_BYTES),
        cost_estimate=pl.CostEstimate(
            flops=4 * count * length * tiles * pair, bytes_accessed=3 << 20, transcendentals=0
        ),
        name="convolve",
    )(turned, spectrum, table)


def gate_kernel(conv_ref, mixed_ref, query_ref, skip_ref, gated_ref):
    conv = conv_ref[...].T.astype(jnp.float32)
    combined = conv + skip_ref[...] * mixed_ref[...].astype(jnp.float32)
    gated_ref[...] = (query_ref[...].astype(jnp.float32) * combined).astype(jnp.bfloat16)


def gate(conv_turned, mixed, query_gate, skip_gain):
    length, width = mixed.shape
    return pl.pallas_call(
        gate_kernel,
        out_shape=jax.ShapeDtypeStruct((length, width), jnp.bfloat16),
        compiler_params=PARAMS,
        cost_estimate=pl.CostEstimate(flops=4 * length * width, bytes_accessed=8 * length * width, transcendentals=0),
        name="gate",
    )(conv_turned, mixed, query_gate, skip_gain.reshape(1, width))


def weights_kernel(number, blocks_ref, weight_ref, own_ref, partner_ref, sems):
    width = weight_ref.shape[0]
    copies = []
    for k in range(number):
        for at, ref in enumerate((partner_ref, own_ref)):
            start = pl.multiple_of(blocks_ref[number * at + k] * width, width)
            copies.append(
                pltpu.make_async_copy(weight_ref.at[:, pl.ds(start, width)], ref.at[k], sems.at[number * at + k])
            )
    for copy in copies:
        copy.start()
    for copy in copies:
        copy.wait()


def weight_blocks(blocks, out_weight):
    width = out_weight.shape[0]
    number = blocks.shape[0] // 2
    shape = jax.ShapeDtypeStruct((number, width, width), jnp.bfloat16)
    return pl.pallas_call(
        functools.partial(weights_kernel, number),
        grid_spec=pltpu.PrefetchScalarGridSpec(
            num_scalar_prefetch=1,
            in_specs=[pl.BlockSpec(memory_space=pl.ANY)],
            out_specs=[pl.BlockSpec(memory_space=pltpu.VMEM)] * 2,
            scratch_shapes=[pltpu.SemaphoreType.DMA((2 * number,))],
        ),
        out_shape=[shape] * 2,
        cost_estimate=pl.CostEstimate(flops=0, bytes_accessed=8 << 20, transcendentals=0),
        name="weight_blocks",
    )(blocks, out_weight)


def own_part_kernel(number, gated_ref, weight_ref, out_ref):
    for k in range(number):
        out_ref[k] = jnp.dot(gated_ref[...], weight_ref[k], preferred_element_type=jnp.float32)


def own_part(gated, own_weight):
    length, width = gated.shape
    number = own_weight.shape[0]
    return pl.pallas_call(
        functools.partial(own_part_kernel, number),
        in_specs=[pl.BlockSpec(memory_space=pltpu.VMEM)] * 2,
        out_specs=pl.BlockSpec(memory_space=pltpu.VMEM),
        out_shape=jax.ShapeDtypeStruct((number, length, width), jnp.float32),
        compiler_params=PARAMS,
        cost_estimate=pl.CostEstimate(
            flops=2 * length * width * width * number, bytes_accessed=2 << 20, transcendentals=0
        ),
        name="own_part",
    )(gated, own_weight)


def project_kernel(which, part_ref, other_ref, weight_ref, *outs):
    half = other_ref.shape[0] // 2
    for at, k in enumerate(which):
        total = part_ref[k] + jnp.dot(other_ref[...], weight_ref[k], preferred_element_type=jnp.float32)
        total = total.astype(jnp.bfloat16)
        outs[2 * at][...] = total[:half]
        outs[2 * at + 1][...] = total[half:]


def project(which, part, other, other_weight):
    _, length, width = part.shape
    number = len(which)
    return pl.pallas_call(
        functools.partial(project_kernel, which),
        in_specs=[pl.BlockSpec(memory_space=pltpu.VMEM)] * 3,
        out_specs=[pl.BlockSpec(memory_space=pltpu.VMEM)] * (2 * number),
        out_shape=[jax.ShapeDtypeStruct((length // 2, width), jnp.bfloat16)] * (2 * number),
        compiler_params=PARAMS,
        cost_estimate=pl.CostEstimate(
            flops=2 * length * width * width * number, bytes_accessed=number << 20, transcendentals=0
        ),
        name="project",
    )(part, other, other_weight)


def finish_kernel(*refs):
    out_ref, out, sems = refs[6:]
    half = refs[0].shape[0]
    size = half // 2

    def put(k):
        part = pl.ds(k * size, size)
        return pltpu.make_async_copy(out.at[part], out_ref.at[part], sems.at[k])

    for k in range(4):
        rows = slice(k % 2 * size, (k % 2 + 1) * size)
        total = sum(ref[rows, :].astype(jnp.float32) for ref in refs[3 * (k // 2) : 3 * (k // 2) + 3])
        out[k * size : (k + 1) * size, :] = total.astype(jnp.bfloat16)
        put(k).start()
    for k in range(4):
        put(k).wait()


def finish(low, high):
    half, width = low[0].shape
    return pl.pallas_call(
        finish_kernel,
        in_specs=[pl.BlockSpec(memory_space=pltpu.VMEM)] * 6,
        out_specs=pl.BlockSpec(memory_space=pl.ANY),
        out_shape=jax.ShapeDtypeStruct((2 * half, width), jnp.bfloat16),
        scratch_shapes=[pltpu.VMEM((2 * half, width), jnp.bfloat16), pltpu.SemaphoreType.DMA((4,))],
        compiler_params=PARAMS,
        cost_estimate=pl.CostEstimate(flops=6 * half * width, bytes_accessed=16 * half * width, transcendentals=0),
        name="finish",
    )(*low, *high)


def added(one, two):
    return (one.astype(jnp.float32) + two.astype(jnp.float32)).astype(jnp.bfloat16)


def body(query_gate, key_gate, value_in, filter_taps, skip_gain, out_weight):
    length, width = query_gate.shape
    ctx, groups = lax.axis_size("ctx"), lax.axis_size("ch")
    ring = groups // CORES
    few = width // ctx
    here, group = lax.axis_index("ctx"), lax.axis_index("ch")
    y, core = group // CORES, group % CORES
    per_tile = LANES // few
    table = jnp.asarray(odd_tables(length))

    def ch_shift(block, dy, dcore):
        route = [(i, ((i // CORES + dy) % ring) * CORES + (i % CORES + dcore) % CORES) for i in range(groups)]
        return lax.ppermute(block, "ch", route)

    mixed, turned = mix(key_gate, value_in)
    place = jnp.stack([here // per_tile, here % per_tile]).astype(jnp.int32)
    spectrum = taps_spectrum(place, filter_taps, table, few)
    ahead = [(y + step) % ring for step in (2, 1, 3, 0)]
    blocks = jnp.stack([k * CORES + at for at in (1 - core, core) for k in ahead]).astype(jnp.int32)
    own_weight, partner_weight = weight_blocks(blocks, out_weight)
    other_weight = ch_shift(partner_weight, 0, 1)

    long_rows = lax.all_to_all(turned.reshape(ctx, few, length), "ctx", 0, 0)
    conv_rows = convolve(long_rows.reshape(ctx * few, length), spectrum, table, few)
    conv_turned = lax.all_to_all(conv_rows.reshape(ctx, few, length), "ctx", 0, 0).reshape(width, length)

    gated = gate(conv_turned, mixed, query_gate, skip_gain)
    other = ch_shift(gated, 0, 1)
    part = own_part(gated, own_weight)
    across_low, across_high = project((0,), part, other, other_weight)
    got_low = ch_shift(across_low, 1, 0)
    got_high = ch_shift(across_high, -1, 0)
    up_low, up_high, down_low, down_high, own_low, own_high = project((1, 2, 3), part, other, other_weight)
    from_below_high = ch_shift(up_high, 1, 0)
    from_above_low = ch_shift(down_low, -1, 0)
    from_below_low = ch_shift(added(up_low, got_low), 1, 0)
    from_above_high = ch_shift(added(down_high, got_high), -1, 0)
    return finish((own_low, from_above_low, from_below_low), (own_high, from_below_high, from_above_high))


def solution(mesh):
    in_specs = (
        P("ctx", "ch"),
        P("ctx", "ch"),
        P("ctx", "ch"),
        P(None, "ch"),
        P("ch"),
        P("ch", None),
    )
    out_specs = P("ctx", "ch")
    return jax.shard_map(body, mesh=mesh, in_specs=in_specs, out_specs=out_specs, check_vma=False)
```

```python
import functools

import jax
import jax.numpy as jnp
import numpy as np
from jax import lax
from jax.experimental import pallas as pl
from jax.experimental.pallas import tpu as pltpu
from jax.sharding import PartitionSpec as P

WIN = 8
LANES = 128
CORES = 2
CONV_BYTES = 53 << 20
PARAMS = pltpu.CompilerParams(vmem_limit_bytes=20 << 20)


def odd_tables(length):
    order = np.concatenate([np.arange(0, length, 2), np.arange(1, length, 2)])
    turns = (np.arange(length)[:, None] * (2 * order[None, :] + 1)) % (4 * length)
    angle = turns * (np.pi / (2 * length))
    tiles = length // LANES
    cos_part = np.cos(angle).reshape(length, tiles, LANES)
    sin_part = -np.sin(angle).reshape(length, tiles, LANES)
    table = np.concatenate([cos_part, sin_part], axis=2).transpose(1, 0, 2)
    return table.astype(jnp.bfloat16)


def mix_kernel(chunks, key_ref, value_ref, mixed_ref, turned_ref, keys, values, sems):
    size = key_ref.shape[0] // chunks

    def fetch(k):
        rows = pl.ds(k * size, size)
        return (
            pltpu.make_async_copy(key_ref.at[rows], keys.at[rows], sems.at[0, k]),
            pltpu.make_async_copy(value_ref.at[rows], values.at[rows], sems.at[1, k]),
        )

    for k in range(chunks):
        for copy in fetch(k):
            copy.start()
    for k in range(chunks):
        for copy in fetch(k):
            copy.wait()
        rows = slice(k * size, (k + 1) * size)
        product = (keys[rows, :].astype(jnp.float32) * values[rows, :].astype(jnp.float32)).astype(jnp.bfloat16)
        mixed_ref[rows, :] = product
        turned_ref[:, rows] = product.T


def mix(key_gate, value_in):
    length, width = key_gate.shape
    chunks = length // LANES
    return pl.pallas_call(
        functools.partial(mix_kernel, chunks),
        in_specs=[pl.BlockSpec(memory_space=pl.ANY)] * 2,
        out_specs=[pl.BlockSpec(memory_space=pltpu.VMEM)] * 2,
        out_shape=[
            jax.ShapeDtypeStruct((length, width), jnp.bfloat16),
            jax.ShapeDtypeStruct((width, length), jnp.bfloat16),
        ],
        scratch_shapes=[pltpu.VMEM((length, width), jnp.bfloat16)] * 2 + [pltpu.SemaphoreType.DMA((2, chunks))],
        cost_estimate=pl.CostEstimate(flops=length * width, bytes_accessed=8 * length * width, transcendentals=0),
        name="mix",
    )(key_gate, value_in)


def taps_kernel(few, place_ref, taps_ref, out_ref, taps, sems):
    length = out_ref.shape[1]
    column = pl.multiple_of(place_ref[0] * LANES, LANES)

    def fetch(k):
        rows = pl.ds(k * length, length)
        return pltpu.make_async_copy(taps_ref.at[rows, pl.ds(column, LANES)], taps.at[rows], sems.at[k])

    for k in range(WIN):
        fetch(k).start()
    first = place_ref[1] * few
    rows = lax.broadcasted_iota(jnp.int32, (few, LANES), 0)
    lanes = lax.broadcasted_iota(jnp.int32, (few, LANES), 1)
    pick = (lanes == rows + first).astype(jnp.bfloat16)
    for k in range(WIN):
        fetch(k).wait()
        picked = lax.dot_general(
            pick,
            taps[k * length : (k + 1) * length, :].astype(jnp.bfloat16),
            (((1,), (1,)), ((), ())),
            preferred_element_type=jnp.float32,
        )
        out_ref[k * few : (k + 1) * few, :] = picked.astype(jnp.bfloat16)


def turned_taps(place, filter_taps, few):
    length = filter_taps.shape[0] // WIN
    return pl.pallas_call(
        functools.partial(taps_kernel, few),
        grid_spec=pltpu.PrefetchScalarGridSpec(
            num_scalar_prefetch=1,
            in_specs=[pl.BlockSpec(memory_space=pl.ANY)],
            out_specs=pl.BlockSpec(memory_space=pltpu.VMEM),
            scratch_shapes=[pltpu.VMEM((WIN * length, LANES), jnp.float32), pltpu.SemaphoreType.DMA((WIN,))],
        ),
        out_shape=jax.ShapeDtypeStruct((WIN * few, length), jnp.bfloat16),
        cost_estimate=pl.CostEstimate(
            flops=2 * few * LANES * WIN * length, bytes_accessed=2 << 20, transcendentals=0
        ),
        name="turned_taps",
    )(place, filter_taps)


def conv_kernel(few, x_ref, taps_ref, table_ref, out_ref, window, product):
    tiles, length, pair = table_ref.shape
    count = x_ref.shape[0]
    spans = count // few

    for tile in range(tiles):
        spectrum = jnp.dot(x_ref[...], table_ref[tile], preferred_element_type=jnp.float32)
        taps = jnp.dot(taps_ref[...], table_ref[tile], preferred_element_type=jnp.float32)
        sign = 1.0 if tile < tiles // 2 else -1.0
        for span in range(spans):
            now = slice(span * few, (span + 1) * few)
            window_real = sign * spectrum[now, LANES:]
            window_imag = -sign * spectrum[now, :LANES]
            if span > 0:
                before = slice((span - 1) * few, span * few)
                window_real = spectrum[before, :LANES] + window_real
                window_imag = spectrum[before, LANES:] + window_imag
            window[tile, 0, now, :] = window_real
            window[tile, 1, now, :] = window_imag
            window[tile, 2, now, :] = window_real + window_imag
        first, plus, minus = [], [], []
        for lag in range(WIN):
            h_real = (-sign / length) * taps[lag * few : (lag + 1) * few, :LANES]
            h_imag = (-sign / length) * taps[lag * few : (lag + 1) * few, LANES:]
            first.append(h_real)
            plus.append(h_real + h_imag)
            minus.append(h_imag - h_real)
        for low in range(0, few, 8):
            part = slice(low, low + 8)
            for span in range(spans):
                one = two = three = None
                for lag in range(min(WIN, span + 1)):
                    at = (span - lag) * few + low
                    term_one = first[lag][part] * window[tile, 2, at : at + 8, :]
                    term_two = plus[lag][part] * window[tile, 1, at : at + 8, :]
                    term_three = minus[lag][part] * window[tile, 0, at : at + 8, :]
                    one = term_one if one is None else one + term_one
                    two = term_two if two is None else two + term_two
                    three = term_three if three is None else three + term_three
                at = span * few + low
                product[tile, at : at + 8, :LANES] = (one + three).astype(jnp.bfloat16)
                product[tile, at : at + 8, LANES:] = (two - one).astype(jnp.bfloat16)
    total = None
    for tile in range(tiles):
        term = lax.dot_general(
            product[tile], table_ref[tile], (((1,), (1,)), ((), ())), preferred_element_type=jnp.float32
        )
        total = term if total is None else total + term
    out_ref[...] = total.astype(jnp.bfloat16)


def convolve(turned, taps, table, few):
    count, length = turned.shape
    tiles, _, pair = table.shape
    return pl.pallas_call(
        functools.partial(conv_kernel, few),
        in_specs=[pl.BlockSpec(memory_space=pltpu.VMEM)] * 3,
        out_specs=pl.BlockSpec(memory_space=pltpu.VMEM),
        out_shape=jax.ShapeDtypeStruct((count, length), jnp.bfloat16),
        scratch_shapes=[
            pltpu.VMEM((tiles, 3, count, LANES), jnp.float32),
            pltpu.VMEM((tiles, count, pair), jnp.bfloat16),
        ],
        compiler_params=pltpu.CompilerParams(vmem_limit_bytes=CONV_BYTES),
        cost_estimate=pl.CostEstimate(
            flops=4 * count * length * tiles * pair, bytes_accessed=3 << 20, transcendentals=0
        ),
        name="convolve",
    )(turned, taps, table)


def gate_kernel(conv_ref, mixed_ref, query_ref, skip_ref, gated_ref):
    conv = conv_ref[...].T.astype(jnp.float32)
    combined = conv + skip_ref[...] * mixed_ref[...].astype(jnp.float32)
    gated_ref[...] = (query_ref[...].astype(jnp.float32) * combined).astype(jnp.bfloat16)


def gate(conv_turned, mixed, query_gate, skip_gain):
    length, width = mixed.shape
    return pl.pallas_call(
        gate_kernel,
        out_shape=jax.ShapeDtypeStruct((length, width), jnp.bfloat16),
        compiler_params=PARAMS,
        cost_estimate=pl.CostEstimate(flops=4 * length * width, bytes_accessed=8 * length * width, transcendentals=0),
        name="gate",
    )(conv_turned, mixed, query_gate, skip_gain.reshape(1, width))


def weights_kernel(number, blocks_ref, weight_ref, own_ref, partner_ref, sems):
    width = weight_ref.shape[0]
    copies = []
    for k in range(number):
        for at, ref in enumerate((partner_ref, own_ref)):
            start = pl.multiple_of(blocks_ref[number * at + k] * width, width)
            copies.append(
                pltpu.make_async_copy(weight_ref.at[:, pl.ds(start, width)], ref.at[k], sems.at[number * at + k])
            )
    for copy in copies:
        copy.start()
    for copy in copies:
        copy.wait()


def weight_blocks(blocks, out_weight):
    width = out_weight.shape[0]
    number = blocks.shape[0] // 2
    shape = jax.ShapeDtypeStruct((number, width, width), jnp.bfloat16)
    return pl.pallas_call(
        functools.partial(weights_kernel, number),
        grid_spec=pltpu.PrefetchScalarGridSpec(
            num_scalar_prefetch=1,
            in_specs=[pl.BlockSpec(memory_space=pl.ANY)],
            out_specs=[pl.BlockSpec(memory_space=pltpu.VMEM)] * 2,
            scratch_shapes=[pltpu.SemaphoreType.DMA((2 * number,))],
        ),
        out_shape=[shape] * 2,
        cost_estimate=pl.CostEstimate(flops=0, bytes_accessed=8 << 20, transcendentals=0),
        name="weight_blocks",
    )(blocks, out_weight)


def own_part_kernel(number, gated_ref, weight_ref, out_ref):
    for k in range(number):
        out_ref[k] = jnp.dot(gated_ref[...], weight_ref[k], preferred_element_type=jnp.float32)


def own_part(gated, own_weight):
    length, width = gated.shape
    number = own_weight.shape[0]
    return pl.pallas_call(
        functools.partial(own_part_kernel, number),
        in_specs=[pl.BlockSpec(memory_space=pltpu.VMEM)] * 2,
        out_specs=pl.BlockSpec(memory_space=pltpu.VMEM),
        out_shape=jax.ShapeDtypeStruct((number, length, width), jnp.float32),
        compiler_params=PARAMS,
        cost_estimate=pl.CostEstimate(
            flops=2 * length * width * width * number, bytes_accessed=2 << 20, transcendentals=0
        ),
        name="own_part",
    )(gated, own_weight)


def project_kernel(which, part_ref, other_ref, weight_ref, *outs):
    half = other_ref.shape[0] // 2
    for at, k in enumerate(which):
        total = part_ref[k] + jnp.dot(other_ref[...], weight_ref[k], preferred_element_type=jnp.float32)
        total = total.astype(jnp.bfloat16)
        outs[2 * at][...] = total[:half]
        outs[2 * at + 1][...] = total[half:]


def project(which, part, other, other_weight):
    _, length, width = part.shape
    number = len(which)
    return pl.pallas_call(
        functools.partial(project_kernel, which),
        in_specs=[pl.BlockSpec(memory_space=pltpu.VMEM)] * 3,
        out_specs=[pl.BlockSpec(memory_space=pltpu.VMEM)] * (2 * number),
        out_shape=[jax.ShapeDtypeStruct((length // 2, width), jnp.bfloat16)] * (2 * number),
        compiler_params=PARAMS,
        cost_estimate=pl.CostEstimate(
            flops=2 * length * width * width * number, bytes_accessed=number << 20, transcendentals=0
        ),
        name="project",
    )(part, other, other_weight)


def finish_kernel(*refs):
    out_ref, out, sems = refs[6:]
    half = refs[0].shape[0]
    size = half // 2

    def put(k):
        part = pl.ds(k * size, size)
        return pltpu.make_async_copy(out.at[part], out_ref.at[part], sems.at[k])

    for k in range(4):
        rows = slice(k % 2 * size, (k % 2 + 1) * size)
        total = sum(ref[rows, :].astype(jnp.float32) for ref in refs[3 * (k // 2) : 3 * (k // 2) + 3])
        out[k * size : (k + 1) * size, :] = total.astype(jnp.bfloat16)
        put(k).start()
    for k in range(4):
        put(k).wait()


def finish(low, high):
    half, width = low[0].shape
    return pl.pallas_call(
        finish_kernel,
        in_specs=[pl.BlockSpec(memory_space=pltpu.VMEM)] * 6,
        out_specs=pl.BlockSpec(memory_space=pl.ANY),
        out_shape=jax.ShapeDtypeStruct((2 * half, width), jnp.bfloat16),
        scratch_shapes=[pltpu.VMEM((2 * half, width), jnp.bfloat16), pltpu.SemaphoreType.DMA((4,))],
        compiler_params=PARAMS,
        cost_estimate=pl.CostEstimate(flops=6 * half * width, bytes_accessed=16 * half * width, transcendentals=0),
        name="finish",
    )(*low, *high)


def added(one, two):
    return (one.astype(jnp.float32) + two.astype(jnp.float32)).astype(jnp.bfloat16)


def body(query_gate, key_gate, value_in, filter_taps, skip_gain, out_weight):
    length, width = query_gate.shape
    ctx, groups = lax.axis_size("ctx"), lax.axis_size("ch")
    ring = groups // CORES
    few = width // ctx
    here, group = lax.axis_index("ctx"), lax.axis_index("ch")
    y, core = group // CORES, group % CORES
    per_tile = LANES // few
    table = jnp.asarray(odd_tables(length))

    def ch_shift(block, dy, dcore):
        route = [(i, ((i // CORES + dy) % ring) * CORES + (i % CORES + dcore) % CORES) for i in range(groups)]
        return lax.ppermute(block, "ch", route)

    mixed, turned = mix(key_gate, value_in)
    place = jnp.stack([here // per_tile, here % per_tile]).astype(jnp.int32)
    taps = turned_taps(place, filter_taps, few)
    ahead = [(y + step) % ring for step in (2, 1, 3, 0)]
    blocks = jnp.stack([k * CORES + at for at in (1 - core, core) for k in ahead]).astype(jnp.int32)
    own_weight, partner_weight = weight_blocks(blocks, out_weight)
    other_weight = ch_shift(partner_weight, 0, 1)

    long_rows = lax.all_to_all(turned.reshape(ctx, few, length), "ctx", 0, 0)
    conv_rows = convolve(long_rows.reshape(ctx * few, length), taps, table, few)
    conv_turned = lax.all_to_all(conv_rows.reshape(ctx, few, length), "ctx", 0, 0).reshape(width, length)

    gated = gate(conv_turned, mixed, query_gate, skip_gain)
    other = ch_shift(gated, 0, 1)
    part = own_part(gated, own_weight)
    across_low, across_high = project((0,), part, other, other_weight)
    got_low = ch_shift(across_low, 1, 0)
    got_high = ch_shift(across_high, -1, 0)
    up_low, up_high, down_low, down_high, own_low, own_high = project((1, 2, 3), part, other, other_weight)
    from_below_high = ch_shift(up_high, 1, 0)
    from_above_low = ch_shift(down_low, -1, 0)
    from_below_low = ch_shift(added(up_low, got_low), 1, 0)
    from_above_high = ch_shift(added(down_high, got_high), -1, 0)
    return finish((own_low, from_above_low, from_below_low), (own_high, from_below_high, from_above_high))


def solution(mesh):
    in_specs = (
        P("ctx", "ch"),
        P("ctx", "ch"),
        P("ctx", "ch"),
        P(None, "ch"),
        P("ch"),
        P("ch", None),
    )
    out_specs = P("ctx", "ch")
    return jax.shard_map(body, mesh=mesh, in_specs=in_specs, out_specs=out_specs, check_vma=False)
```

```python
import functools

import jax
import jax.numpy as jnp
import numpy as np
from jax import lax
from jax.experimental import pallas as pl
from jax.experimental.pallas import tpu as pltpu
from jax.sharding import PartitionSpec as P

WIN = 8
LANES = 128
CORES = 2
CONV_BYTES = 54400 << 10
PARAMS = pltpu.CompilerParams(vmem_limit_bytes=20 << 20)


def odd_tables(length):
    order = np.concatenate([np.arange(0, length, 2), np.arange(1, length, 2)])
    turns = (np.arange(length)[:, None] * (2 * order[None, :] + 1)) % (4 * length)
    angle = turns * (np.pi / (2 * length))
    tiles = length // LANES
    cos_part = np.cos(angle).reshape(length, tiles, LANES)
    sin_part = -np.sin(angle).reshape(length, tiles, LANES)
    table = np.concatenate([cos_part, sin_part], axis=2).transpose(1, 0, 2)
    return table.astype(jnp.bfloat16)


def mix_kernel(chunks, key_ref, value_ref, mixed_ref, turned_ref, keys, values, sems):
    size = key_ref.shape[0] // chunks

    def fetch(k):
        rows = pl.ds(k * size, size)
        return (
            pltpu.make_async_copy(key_ref.at[rows], keys.at[rows], sems.at[0, k]),
            pltpu.make_async_copy(value_ref.at[rows], values.at[rows], sems.at[1, k]),
        )

    for k in range(chunks):
        for copy in fetch(k):
            copy.start()
    for k in range(chunks):
        for copy in fetch(k):
            copy.wait()
        rows = slice(k * size, (k + 1) * size)
        product = (keys[rows, :].astype(jnp.float32) * values[rows, :].astype(jnp.float32)).astype(jnp.bfloat16)
        mixed_ref[rows, :] = product
        turned_ref[:, rows] = product.T


def mix(key_gate, value_in):
    length, width = key_gate.shape
    chunks = length // LANES
    return pl.pallas_call(
        functools.partial(mix_kernel, chunks),
        in_specs=[pl.BlockSpec(memory_space=pl.ANY)] * 2,
        out_specs=[pl.BlockSpec(memory_space=pltpu.VMEM)] * 2,
        out_shape=[
            jax.ShapeDtypeStruct((length, width), jnp.bfloat16),
            jax.ShapeDtypeStruct((width, length), jnp.bfloat16),
        ],
        scratch_shapes=[pltpu.VMEM((length, width), jnp.bfloat16)] * 2 + [pltpu.SemaphoreType.DMA((2, chunks))],
        cost_estimate=pl.CostEstimate(flops=length * width, bytes_accessed=8 * length * width, transcendentals=0),
        name="mix",
    )(key_gate, value_in)


def taps_kernel(few, place_ref, taps_ref, out_ref, taps, out, sems):
    length = out_ref.shape[1]
    column = pl.multiple_of(place_ref[0] * LANES, LANES)

    def fetch(k):
        rows = pl.ds(k * length, length)
        return pltpu.make_async_copy(taps_ref.at[rows, pl.ds(column, LANES)], taps.at[rows], sems.at[k])

    for k in range(WIN):
        fetch(k).start()
    first = place_ref[1] * few
    rows = lax.broadcasted_iota(jnp.int32, (few, LANES), 0)
    lanes = lax.broadcasted_iota(jnp.int32, (few, LANES), 1)
    pick = (lanes == rows + first).astype(jnp.bfloat16)
    for k in range(WIN):
        fetch(k).wait()
        picked = lax.dot_general(
            pick,
            taps[k * length : (k + 1) * length, :].astype(jnp.bfloat16),
            (((1,), (1,)), ((), ())),
            preferred_element_type=jnp.float32,
        )
        out[k * few : (k + 1) * few, :] = picked.astype(jnp.bfloat16)
    put = pltpu.make_async_copy(out, out_ref.at[pl.ds(0, WIN * few)], sems.at[WIN])
    put.start()
    put.wait()


def turned_taps(place, filter_taps, few):
    length = filter_taps.shape[0] // WIN
    return pl.pallas_call(
        functools.partial(taps_kernel, few),
        grid_spec=pltpu.PrefetchScalarGridSpec(
            num_scalar_prefetch=1,
            in_specs=[pl.BlockSpec(memory_space=pl.ANY)],
            out_specs=pl.BlockSpec(memory_space=pl.ANY),
            scratch_shapes=[
                pltpu.VMEM((WIN * length, LANES), jnp.float32),
                pltpu.VMEM((WIN * few, length), jnp.bfloat16),
                pltpu.SemaphoreType.DMA((WIN + 1,)),
            ],
        ),
        out_shape=jax.ShapeDtypeStruct((length, length), jnp.bfloat16),
        cost_estimate=pl.CostEstimate(
            flops=2 * few * LANES * WIN * length, bytes_accessed=2 << 20, transcendentals=0
        ),
        name="turned_taps",
    )(place, filter_taps)


def conv_kernel(few, x_ref, taps_ref, table_ref, out_ref, rows, tap_rows, table, window, product, sems):
    tiles, length, pair = table_ref.shape
    count = x_ref.shape[0]
    spans = count // few

    copies = [
        pltpu.make_async_copy(x_ref, rows, sems.at[0]),
        pltpu.make_async_copy(taps_ref.at[pl.ds(0, WIN * few)], tap_rows, sems.at[1]),
        pltpu.make_async_copy(table_ref, table, sems.at[2]),
    ]
    for copy in copies:
        copy.start()
    for copy in copies:
        copy.wait()
    for tile in range(tiles):
        spectrum = jnp.dot(rows[...], table[tile], preferred_element_type=jnp.float32)
        taps = jnp.dot(tap_rows[...], table[tile], preferred_element_type=jnp.float32)
        sign = 1.0 if tile < tiles // 2 else -1.0
        for span in range(spans):
            now = slice(span * few, (span + 1) * few)
            window_real = sign * spectrum[now, LANES:]
            window_imag = -sign * spectrum[now, :LANES]
            if span > 0:
                before = slice((span - 1) * few, span * few)
                window_real = spectrum[before, :LANES] + window_real
                window_imag = spectrum[before, LANES:] + window_imag
            window[tile, 0, now, :] = window_real
            window[tile, 1, now, :] = window_imag
            window[tile, 2, now, :] = window_real + window_imag
        first, plus, minus = [], [], []
        for lag in range(WIN):
            h_real = (-sign / length) * taps[lag * few : (lag + 1) * few, :LANES]
            h_imag = (-sign / length) * taps[lag * few : (lag + 1) * few, LANES:]
            first.append(h_real)
            plus.append(h_real + h_imag)
            minus.append(h_imag - h_real)
        for low in range(0, few, 8):
            part = slice(low, low + 8)
            for span in range(spans):
                one = two = three = None
                for lag in range(min(WIN, span + 1)):
                    at = (span - lag) * few + low
                    term_one = first[lag][part] * window[tile, 2, at : at + 8, :]
                    term_two = plus[lag][part] * window[tile, 1, at : at + 8, :]
                    term_three = minus[lag][part] * window[tile, 0, at : at + 8, :]
                    one = term_one if one is None else one + term_one
                    two = term_two if two is None else two + term_two
                    three = term_three if three is None else three + term_three
                at = span * few + low
                product[tile, at : at + 8, :LANES] = (one + three).astype(jnp.bfloat16)
                product[tile, at : at + 8, LANES:] = (two - one).astype(jnp.bfloat16)
    total = None
    for tile in range(tiles):
        term = lax.dot_general(
            product[tile], table[tile], (((1,), (1,)), ((), ())), preferred_element_type=jnp.float32
        )
        total = term if total is None else total + term
    out_ref[...] = total.astype(jnp.bfloat16)


def convolve(turned, taps, table, few):
    count, length = turned.shape
    tiles, _, pair = table.shape
    return pl.pallas_call(
        functools.partial(conv_kernel, few),
        in_specs=[pl.BlockSpec(memory_space=pl.ANY)] * 3,
        out_specs=pl.BlockSpec(memory_space=pltpu.VMEM),
        out_shape=jax.ShapeDtypeStruct((count, length), jnp.bfloat16),
        scratch_shapes=[
            pltpu.VMEM((count, length), jnp.bfloat16),
            pltpu.VMEM((WIN * few, length), jnp.bfloat16),
            pltpu.VMEM(table.shape, jnp.bfloat16),
            pltpu.VMEM((tiles, 3, count, LANES), jnp.float32),
            pltpu.VMEM((tiles, count, pair), jnp.bfloat16),
            pltpu.SemaphoreType.DMA((3,)),
        ],
        compiler_params=pltpu.CompilerParams(vmem_limit_bytes=CONV_BYTES),
        cost_estimate=pl.CostEstimate(
            flops=4 * count * length * tiles * pair, bytes_accessed=3 << 20, transcendentals=0
        ),
        name="convolve",
    )(turned, taps, table)


def gate_kernel(conv_ref, mixed_ref, query_ref, skip_ref, gated_ref):
    conv = conv_ref[...].T.astype(jnp.float32)
    combined = conv + skip_ref[...] * mixed_ref[...].astype(jnp.float32)
    gated_ref[...] = (query_ref[...].astype(jnp.float32) * combined).astype(jnp.bfloat16)


def gate(conv_turned, mixed, query_gate, skip_gain):
    length, width = mixed.shape
    return pl.pallas_call(
        gate_kernel,
        out_shape=jax.ShapeDtypeStruct((length, width), jnp.bfloat16),
        compiler_params=PARAMS,
        cost_estimate=pl.CostEstimate(flops=4 * length * width, bytes_accessed=8 * length * width, transcendentals=0),
        name="gate",
    )(conv_turned, mixed, query_gate, skip_gain.reshape(1, width))


def weights_kernel(number, blocks_ref, weight_ref, own_ref, partner_ref, sems):
    width = weight_ref.shape[0]
    copies = []
    for k in range(number):
        for at, ref in enumerate((partner_ref, own_ref)):
            start = pl.multiple_of(blocks_ref[number * at + k] * width, width)
            copies.append(
                pltpu.make_async_copy(weight_ref.at[:, pl.ds(start, width)], ref.at[k], sems.at[number * at + k])
            )
    for copy in copies:
        copy.start()
    for copy in copies:
        copy.wait()


def weight_blocks(blocks, out_weight):
    width = out_weight.shape[0]
    number = blocks.shape[0] // 2
    shape = jax.ShapeDtypeStruct((number, width, width), jnp.bfloat16)
    return pl.pallas_call(
        functools.partial(weights_kernel, number),
        grid_spec=pltpu.PrefetchScalarGridSpec(
            num_scalar_prefetch=1,
            in_specs=[pl.BlockSpec(memory_space=pl.ANY)],
            out_specs=[pl.BlockSpec(memory_space=pltpu.VMEM)] * 2,
            scratch_shapes=[pltpu.SemaphoreType.DMA((2 * number,))],
        ),
        out_shape=[shape] * 2,
        cost_estimate=pl.CostEstimate(flops=0, bytes_accessed=8 << 20, transcendentals=0),
        name="weight_blocks",
    )(blocks, out_weight)


def own_part_kernel(number, gated_ref, weight_ref, out_ref):
    for k in range(number):
        out_ref[k] = jnp.dot(gated_ref[...], weight_ref[k], preferred_element_type=jnp.float32)


def own_part(gated, own_weight):
    length, width = gated.shape
    number = own_weight.shape[0]
    return pl.pallas_call(
        functools.partial(own_part_kernel, number),
        in_specs=[pl.BlockSpec(memory_space=pltpu.VMEM)] * 2,
        out_specs=pl.BlockSpec(memory_space=pltpu.VMEM),
        out_shape=jax.ShapeDtypeStruct((number, length, width), jnp.float32),
        compiler_params=PARAMS,
        cost_estimate=pl.CostEstimate(
            flops=2 * length * width * width * number, bytes_accessed=2 << 20, transcendentals=0
        ),
        name="own_part",
    )(gated, own_weight)


def project_kernel(which, part_ref, other_ref, weight_ref, *outs):
    half = other_ref.shape[0] // 2
    for at, k in enumerate(which):
        total = part_ref[k] + jnp.dot(other_ref[...], weight_ref[k], preferred_element_type=jnp.float32)
        total = total.astype(jnp.bfloat16)
        outs[2 * at][...] = total[:half]
        outs[2 * at + 1][...] = total[half:]


def project(which, part, other, other_weight):
    _, length, width = part.shape
    number = len(which)
    return pl.pallas_call(
        functools.partial(project_kernel, which),
        in_specs=[pl.BlockSpec(memory_space=pltpu.VMEM)] * 3,
        out_specs=[pl.BlockSpec(memory_space=pltpu.VMEM)] * (2 * number),
        out_shape=[jax.ShapeDtypeStruct((length // 2, width), jnp.bfloat16)] * (2 * number),
        compiler_params=PARAMS,
        cost_estimate=pl.CostEstimate(
            flops=2 * length * width * width * number, bytes_accessed=number << 20, transcendentals=0
        ),
        name="project",
    )(part, other, other_weight)


def finish_kernel(*refs):
    out_ref, out, sems = refs[6:]
    half = refs[0].shape[0]
    size = half // 2

    def put(k):
        part = pl.ds(k * size, size)
        return pltpu.make_async_copy(out.at[part], out_ref.at[part], sems.at[k])

    for k in range(4):
        rows = slice(k % 2 * size, (k % 2 + 1) * size)
        total = sum(ref[rows, :].astype(jnp.float32) for ref in refs[3 * (k // 2) : 3 * (k // 2) + 3])
        out[k * size : (k + 1) * size, :] = total.astype(jnp.bfloat16)
        put(k).start()
    for k in range(4):
        put(k).wait()


def finish(low, high):
    half, width = low[0].shape
    return pl.pallas_call(
        finish_kernel,
        in_specs=[pl.BlockSpec(memory_space=pltpu.VMEM)] * 6,
        out_specs=pl.BlockSpec(memory_space=pl.ANY),
        out_shape=jax.ShapeDtypeStruct((2 * half, width), jnp.bfloat16),
        scratch_shapes=[pltpu.VMEM((2 * half, width), jnp.bfloat16), pltpu.SemaphoreType.DMA((4,))],
        compiler_params=PARAMS,
        cost_estimate=pl.CostEstimate(flops=6 * half * width, bytes_accessed=16 * half * width, transcendentals=0),
        name="finish",
    )(*low, *high)


def added(one, two):
    return (one.astype(jnp.float32) + two.astype(jnp.float32)).astype(jnp.bfloat16)


def body(query_gate, key_gate, value_in, filter_taps, skip_gain, out_weight):
    length, width = query_gate.shape
    ctx, groups = lax.axis_size("ctx"), lax.axis_size("ch")
    ring = groups // CORES
    few = width // ctx
    here, group = lax.axis_index("ctx"), lax.axis_index("ch")
    y, core = group // CORES, group % CORES
    per_tile = LANES // few
    table = jnp.asarray(odd_tables(length))

    def ch_shift(block, dy, dcore):
        route = [(i, ((i // CORES + dy) % ring) * CORES + (i % CORES + dcore) % CORES) for i in range(groups)]
        return lax.ppermute(block, "ch", route)

    mixed, turned = mix(key_gate, value_in)
    place = jnp.stack([here // per_tile, here % per_tile]).astype(jnp.int32)
    taps = turned_taps(place, filter_taps, few)
    ahead = [(y + step) % ring for step in (2, 1, 3, 0)]
    blocks = jnp.stack([k * CORES + at for at in (1 - core, core) for k in ahead]).astype(jnp.int32)
    own_weight, partner_weight = weight_blocks(blocks, out_weight)
    other_weight = ch_shift(partner_weight, 0, 1)

    long_rows = lax.all_to_all(turned.reshape(ctx, few, length), "ctx", 0, 0)
    conv_rows = convolve(long_rows.reshape(ctx * few, length), taps, table, few)
    conv_turned = lax.all_to_all(conv_rows.reshape(ctx, few, length), "ctx", 0, 0).reshape(width, length)

    gated = gate(conv_turned, mixed, query_gate, skip_gain)
    other = ch_shift(gated, 0, 1)
    part = own_part(gated, own_weight)
    across_low, across_high, up_low, up_high, down_low, down_high, own_low, own_high = project(
        (0, 1, 2, 3), part, other, other_weight
    )
    got_low = ch_shift(across_low, 1, 0)
    got_high = ch_shift(across_high, -1, 0)
    from_below_high = ch_shift(up_high, 1, 0)
    from_above_low = ch_shift(down_low, -1, 0)
    from_below_low = ch_shift(added(up_low, got_low), 1, 0)
    from_above_high = ch_shift(added(down_high, got_high), -1, 0)
    return finish((own_low, from_above_low, from_below_low), (own_high, from_below_high, from_above_high))


def solution(mesh):
    in_specs = (
        P("ctx", "ch"),
        P("ctx", "ch"),
        P("ctx", "ch"),
        P(None, "ch"),
        P("ch"),
        P("ch", None),
    )
    out_specs = P("ctx", "ch")
    return jax.shard_map(body, mesh=mesh, in_specs=in_specs, out_specs=out_specs, check_vma=False)
```

```python
import functools

import jax
import jax.numpy as jnp
import numpy as np
from jax import lax
from jax.experimental import pallas as pl
from jax.experimental.pallas import tpu as pltpu
from jax.sharding import PartitionSpec as P

WIN = 8
LANES = 128
CORES = 2
CONV_BYTES = 54400 << 10
PARAMS = pltpu.CompilerParams(vmem_limit_bytes=20 << 20)


def odd_tables(length):
    order = np.concatenate([np.arange(0, length, 2), np.arange(1, length, 2)])
    turns = (np.arange(length)[:, None] * (2 * order[None, :] + 1)) % (4 * length)
    angle = turns * (np.pi / (2 * length))
    tiles = length // LANES
    cos_part = np.cos(angle).reshape(length, tiles, LANES)
    sin_part = -np.sin(angle).reshape(length, tiles, LANES)
    table = np.concatenate([cos_part, sin_part], axis=2).transpose(1, 0, 2)
    return table.astype(jnp.bfloat16)


def mix_kernel(chunks, key_ref, value_ref, mixed_ref, turned_ref, keys, values, sems):
    size = key_ref.shape[0] // chunks

    def fetch(k):
        rows = pl.ds(k * size, size)
        return (
            pltpu.make_async_copy(key_ref.at[rows], keys.at[rows], sems.at[0, k]),
            pltpu.make_async_copy(value_ref.at[rows], values.at[rows], sems.at[1, k]),
        )

    for k in range(chunks):
        for copy in fetch(k):
            copy.start()
    for k in range(chunks):
        for copy in fetch(k):
            copy.wait()
        rows = slice(k * size, (k + 1) * size)
        product = (keys[rows, :].astype(jnp.float32) * values[rows, :].astype(jnp.float32)).astype(jnp.bfloat16)
        mixed_ref[rows, :] = product
        turned_ref[:, rows] = product.T


def mix(key_gate, value_in):
    length, width = key_gate.shape
    chunks = length // LANES
    return pl.pallas_call(
        functools.partial(mix_kernel, chunks),
        in_specs=[pl.BlockSpec(memory_space=pl.ANY)] * 2,
        out_specs=[pl.BlockSpec(memory_space=pltpu.VMEM)] * 2,
        out_shape=[
            jax.ShapeDtypeStruct((length, width), jnp.bfloat16),
            jax.ShapeDtypeStruct((width, length), jnp.bfloat16),
        ],
        scratch_shapes=[pltpu.VMEM((length, width), jnp.bfloat16)] * 2 + [pltpu.SemaphoreType.DMA((2, chunks))],
        cost_estimate=pl.CostEstimate(flops=length * width, bytes_accessed=8 * length * width, transcendentals=0),
        name="mix",
    )(key_gate, value_in)


def taps_kernel(few, place_ref, taps_ref, out_ref, taps, out, sems):
    length = out_ref.shape[1]
    column = pl.multiple_of(place_ref[0] * LANES, LANES)

    def fetch(k):
        rows = pl.ds(k * length, length)
        return pltpu.make_async_copy(taps_ref.at[rows, pl.ds(column, LANES)], taps.at[rows], sems.at[k])

    for k in range(WIN):
        fetch(k).start()
    first = place_ref[1] * few
    rows = lax.broadcasted_iota(jnp.int32, (few, LANES), 0)
    lanes = lax.broadcasted_iota(jnp.int32, (few, LANES), 1)
    pick = (lanes == rows + first).astype(jnp.bfloat16)
    for k in range(WIN):
        fetch(k).wait()
        picked = lax.dot_general(
            pick,
            taps[k * length : (k + 1) * length, :].astype(jnp.bfloat16),
            (((1,), (1,)), ((), ())),
            preferred_element_type=jnp.float32,
        )
        out[k * few : (k + 1) * few, :] = picked.astype(jnp.bfloat16)
    put = pltpu.make_async_copy(out, out_ref.at[pl.ds(0, WIN * few)], sems.at[WIN])
    put.start()
    put.wait()


def turned_taps(place, filter_taps, few):
    length = filter_taps.shape[0] // WIN
    return pl.pallas_call(
        functools.partial(taps_kernel, few),
        grid_spec=pltpu.PrefetchScalarGridSpec(
            num_scalar_prefetch=1,
            in_specs=[pl.BlockSpec(memory_space=pl.ANY)],
            out_specs=pl.BlockSpec(memory_space=pl.ANY),
            scratch_shapes=[
                pltpu.VMEM((WIN * length, LANES), jnp.float32),
                pltpu.VMEM((WIN * few, length), jnp.bfloat16),
                pltpu.SemaphoreType.DMA((WIN + 1,)),
            ],
        ),
        out_shape=jax.ShapeDtypeStruct((length, length), jnp.bfloat16),
        cost_estimate=pl.CostEstimate(
            flops=2 * few * LANES * WIN * length, bytes_accessed=2 << 20, transcendentals=0
        ),
        name="turned_taps",
    )(place, filter_taps)


def conv_kernel(few, x_ref, taps_ref, table_ref, out_ref, rows, tap_rows, table, window, product, sems):
    tiles, length, pair = table_ref.shape
    count = x_ref.shape[0]
    spans = count // few

    copies = [
        pltpu.make_async_copy(x_ref, rows, sems.at[0]),
        pltpu.make_async_copy(taps_ref.at[pl.ds(0, WIN * few)], tap_rows, sems.at[1]),
        pltpu.make_async_copy(table_ref, table, sems.at[2]),
    ]
    for copy in copies:
        copy.start()
    for copy in copies:
        copy.wait()
    for tile in range(tiles):
        spectrum = jnp.dot(rows[...], table[tile], preferred_element_type=jnp.float32)
        taps = jnp.dot(tap_rows[...], table[tile], preferred_element_type=jnp.float32)
        sign = 1.0 if tile < tiles // 2 else -1.0
        for span in range(spans):
            now = slice(span * few, (span + 1) * few)
            window_real = sign * spectrum[now, LANES:]
            window_imag = -sign * spectrum[now, :LANES]
            if span > 0:
                before = slice((span - 1) * few, span * few)
                window_real = spectrum[before, :LANES] + window_real
                window_imag = spectrum[before, LANES:] + window_imag
            window[tile, 0, now, :] = window_real
            window[tile, 1, now, :] = window_imag
            window[tile, 2, now, :] = window_real + window_imag
        first, plus, minus = [], [], []
        for lag in range(WIN):
            h_real = (-sign / length) * taps[lag * few : (lag + 1) * few, :LANES]
            h_imag = (-sign / length) * taps[lag * few : (lag + 1) * few, LANES:]
            first.append(h_real)
            plus.append(h_real + h_imag)
            minus.append(h_imag - h_real)
        for low in range(0, few, 8):
            part = slice(low, low + 8)
            for span in range(spans):
                one = two = three = None
                for lag in range(min(WIN, span + 1)):
                    at = (span - lag) * few + low
                    term_one = first[lag][part] * window[tile, 2, at : at + 8, :]
                    term_two = plus[lag][part] * window[tile, 1, at : at + 8, :]
                    term_three = minus[lag][part] * window[tile, 0, at : at + 8, :]
                    one = term_one if one is None else one + term_one
                    two = term_two if two is None else two + term_two
                    three = term_three if three is None else three + term_three
                at = span * few + low
                product[tile, at : at + 8, :LANES] = (one + three).astype(jnp.bfloat16)
                product[tile, at : at + 8, LANES:] = (two - one).astype(jnp.bfloat16)
    total = None
    for tile in range(tiles):
        term = lax.dot_general(
            product[tile], table[tile], (((1,), (1,)), ((), ())), preferred_element_type=jnp.float32
        )
        total = term if total is None else total + term
    out_ref[...] = total.astype(jnp.bfloat16)


def convolve(turned, taps, table, few):
    count, length = turned.shape
    tiles, _, pair = table.shape
    return pl.pallas_call(
        functools.partial(conv_kernel, few),
        in_specs=[pl.BlockSpec(memory_space=pl.ANY)] * 3,
        out_specs=pl.BlockSpec(memory_space=pltpu.VMEM),
        out_shape=jax.ShapeDtypeStruct((count, length), jnp.bfloat16),
        scratch_shapes=[
            pltpu.VMEM((count, length), jnp.bfloat16),
            pltpu.VMEM((WIN * few, length), jnp.bfloat16),
            pltpu.VMEM(table.shape, jnp.bfloat16),
            pltpu.VMEM((tiles, 3, count, LANES), jnp.float32),
            pltpu.VMEM((tiles, count, pair), jnp.bfloat16),
            pltpu.SemaphoreType.DMA((3,)),
        ],
        compiler_params=pltpu.CompilerParams(vmem_limit_bytes=CONV_BYTES),
        cost_estimate=pl.CostEstimate(
            flops=4 * count * length * tiles * pair, bytes_accessed=3 << 20, transcendentals=0
        ),
        name="convolve",
    )(turned, taps, table)


def gate_kernel(conv_ref, mixed_ref, query_ref, skip_ref, gated_ref):
    conv = conv_ref[...].T.astype(jnp.float32)
    combined = conv + skip_ref[...] * mixed_ref[...].astype(jnp.float32)
    gated_ref[...] = (query_ref[...].astype(jnp.float32) * combined).astype(jnp.bfloat16)


def gate(conv_turned, mixed, query_gate, skip_gain):
    length, width = mixed.shape
    return pl.pallas_call(
        gate_kernel,
        out_shape=jax.ShapeDtypeStruct((length, width), jnp.bfloat16),
        compiler_params=PARAMS,
        cost_estimate=pl.CostEstimate(flops=4 * length * width, bytes_accessed=8 * length * width, transcendentals=0),
        name="gate",
    )(conv_turned, mixed, query_gate, skip_gain.reshape(1, width))


def weights_kernel(number, blocks_ref, weight_ref, own_ref, partner_ref, sems):
    width = weight_ref.shape[0]
    copies = []
    for k in range(number):
        for at, ref in enumerate((partner_ref, own_ref)):
            start = pl.multiple_of(blocks_ref[number * at + k] * width, width)
            copies.append(
                pltpu.make_async_copy(weight_ref.at[:, pl.ds(start, width)], ref.at[k], sems.at[number * at + k])
            )
    for copy in copies:
        copy.start()
    for copy in copies:
        copy.wait()


def weight_blocks(blocks, out_weight):
    width = out_weight.shape[0]
    number = blocks.shape[0] // 2
    shape = jax.ShapeDtypeStruct((number, width, width), jnp.bfloat16)
    return pl.pallas_call(
        functools.partial(weights_kernel, number),
        grid_spec=pltpu.PrefetchScalarGridSpec(
            num_scalar_prefetch=1,
            in_specs=[pl.BlockSpec(memory_space=pl.ANY)],
            out_specs=[pl.BlockSpec(memory_space=pltpu.VMEM)] * 2,
            scratch_shapes=[pltpu.SemaphoreType.DMA((2 * number,))],
        ),
        out_shape=[shape] * 2,
        cost_estimate=pl.CostEstimate(flops=0, bytes_accessed=8 << 20, transcendentals=0),
        name="weight_blocks",
    )(blocks, out_weight)


def own_part_kernel(number, gated_ref, weight_ref, out_ref):
    for k in range(number):
        out_ref[k] = jnp.dot(gated_ref[...], weight_ref[k], preferred_element_type=jnp.float32)


def own_part(gated, own_weight):
    length, width = gated.shape
    number = own_weight.shape[0]
    return pl.pallas_call(
        functools.partial(own_part_kernel, number),
        in_specs=[pl.BlockSpec(memory_space=pltpu.VMEM)] * 2,
        out_specs=pl.BlockSpec(memory_space=pltpu.VMEM),
        out_shape=jax.ShapeDtypeStruct((number, length, width), jnp.float32),
        compiler_params=PARAMS,
        cost_estimate=pl.CostEstimate(
            flops=2 * length * width * width * number, bytes_accessed=2 << 20, transcendentals=0
        ),
        name="own_part",
    )(gated, own_weight)


def project_kernel(which, part_ref, other_ref, weight_ref, *outs):
    half = other_ref.shape[0] // 2
    for at, k in enumerate(which):
        total = part_ref[k] + jnp.dot(other_ref[...], weight_ref[k], preferred_element_type=jnp.float32)
        total = total.astype(jnp.bfloat16)
        outs[2 * at][...] = total[:half]
        outs[2 * at + 1][...] = total[half:]


def project(which, part, other, other_weight):
    _, length, width = part.shape
    number = len(which)
    return pl.pallas_call(
        functools.partial(project_kernel, which),
        in_specs=[pl.BlockSpec(memory_space=pltpu.VMEM)] * 3,
        out_specs=[pl.BlockSpec(memory_space=pltpu.VMEM)] * (2 * number),
        out_shape=[jax.ShapeDtypeStruct((length // 2, width), jnp.bfloat16)] * (2 * number),
        compiler_params=PARAMS,
        cost_estimate=pl.CostEstimate(
            flops=2 * length * width * width * number, bytes_accessed=number << 20, transcendentals=0
        ),
        name="project",
    )(part, other, other_weight)


def finish_kernel(first, one_ref, two_ref, three_ref, *refs):
    out_ref, out, sems = refs[-3:]
    half = one_ref.shape[0]
    size = half // 2
    base = 0 if first else half

    def put(k):
        part = pl.ds(k * size, size)
        return pltpu.make_async_copy(out.at[part], out_ref.at[pl.ds(base + k * size, size)], sems.at[k])

    for k in range(2):
        rows = slice(k * size, (k + 1) * size)
        total = sum(ref[rows, :].astype(jnp.float32) for ref in (one_ref, two_ref, three_ref))
        out[rows, :] = total.astype(jnp.bfloat16)
        put(k).start()
    for k in range(2):
        put(k).wait()


def finish(terms, into=None):
    half, width = terms[0].shape
    first = into is None
    return pl.pallas_call(
        functools.partial(finish_kernel, first),
        in_specs=[pl.BlockSpec(memory_space=pltpu.VMEM)] * 3 + [pl.BlockSpec(memory_space=pl.ANY)] * (not first),
        out_specs=pl.BlockSpec(memory_space=pl.ANY),
        out_shape=jax.ShapeDtypeStruct((2 * half, width), jnp.bfloat16),
        scratch_shapes=[pltpu.VMEM((half, width), jnp.bfloat16), pltpu.SemaphoreType.DMA((2,))],
        input_output_aliases={} if first else {3: 0},
        compiler_params=PARAMS,
        cost_estimate=pl.CostEstimate(flops=3 * half * width, bytes_accessed=8 * half * width, transcendentals=0),
        name="finish",
    )(*terms, *([] if first else [into]))


def added(one, two):
    return (one.astype(jnp.float32) + two.astype(jnp.float32)).astype(jnp.bfloat16)


def body(query_gate, key_gate, value_in, filter_taps, skip_gain, out_weight):
    length, width = query_gate.shape
    ctx, groups = lax.axis_size("ctx"), lax.axis_size("ch")
    ring = groups // CORES
    few = width // ctx
    here, group = lax.axis_index("ctx"), lax.axis_index("ch")
    y, core = group // CORES, group % CORES
    per_tile = LANES // few
    table = jnp.asarray(odd_tables(length))

    def ch_shift(block, dy, dcore):
        route = [(i, ((i // CORES + dy) % ring) * CORES + (i % CORES + dcore) % CORES) for i in range(groups)]
        return lax.ppermute(block, "ch", route)

    mixed, turned = mix(key_gate, value_in)
    place = jnp.stack([here // per_tile, here % per_tile]).astype(jnp.int32)
    taps = turned_taps(place, filter_taps, few)
    ahead = [(y + step) % ring for step in (2, 1, 3, 0)]
    blocks = jnp.stack([k * CORES + at for at in (1 - core, core) for k in ahead]).astype(jnp.int32)
    own_weight, partner_weight = weight_blocks(blocks, out_weight)
    other_weight = ch_shift(partner_weight, 0, 1)

    long_rows = lax.all_to_all(turned.reshape(ctx, few, length), "ctx", 0, 0)
    conv_rows = convolve(long_rows.reshape(ctx * few, length), taps, table, few)
    conv_turned = lax.all_to_all(conv_rows.reshape(ctx, few, length), "ctx", 0, 0).reshape(width, length)

    gated = gate(conv_turned, mixed, query_gate, skip_gain)
    other = ch_shift(gated, 0, 1)
    part = own_part(gated, own_weight)
    across_low, across_high = project((0,), part, other, other_weight)
    got_low = ch_shift(across_low, 1, 0)
    up_low, up_high, down_low, down_high, own_low, own_high = project((1, 2, 3), part, other, other_weight)
    across_high, up_high = lax.optimization_barrier((across_high, up_high))
    got_high = ch_shift(across_high, -1, 0)
    from_below_high = ch_shift(up_high, 1, 0)
    from_above_low = ch_shift(down_low, -1, 0)
    from_below_low = ch_shift(added(up_low, got_low), 1, 0)
    from_above_high = ch_shift(added(down_high, got_high), -1, 0)
    lower = finish((own_low, from_above_low, from_below_low))
    return finish((own_high, from_below_high, from_above_high), lower)


def solution(mesh):
    in_specs = (
        P("ctx", "ch"),
        P("ctx", "ch"),
        P("ctx", "ch"),
        P(None, "ch"),
        P("ch"),
        P("ch", None),
    )
    out_specs = P("ctx", "ch")
    return jax.shard_map(body, mesh=mesh, in_specs=in_specs, out_specs=out_specs, check_vma=False)
```

```python
import functools

import jax
import jax.numpy as jnp
import numpy as np
from jax import lax
from jax.experimental import pallas as pl
from jax.experimental.pallas import tpu as pltpu
from jax.sharding import PartitionSpec as P

WIN = 8
LANES = 128
CORES = 2
CONV_BYTES = 54400 << 10
PARAMS = pltpu.CompilerParams(vmem_limit_bytes=20 << 20)


def odd_tables(length):
    order = np.concatenate([np.arange(0, length, 2), np.arange(1, length, 2)])
    turns = (np.arange(length)[:, None] * (2 * order[None, :] + 1)) % (4 * length)
    angle = turns * (np.pi / (2 * length))
    tiles = length // LANES
    cos_part = np.cos(angle).reshape(length, tiles, LANES)
    sin_part = -np.sin(angle).reshape(length, tiles, LANES)
    table = np.concatenate([cos_part, sin_part], axis=2).transpose(1, 0, 2)
    return table.astype(jnp.bfloat16)


def mix_kernel(chunks, key_ref, value_ref, mixed_ref, turned_ref, keys, values, mixed, turned, sems):
    size = key_ref.shape[0] // chunks

    def fetch(k):
        rows = pl.ds(k * size, size)
        return (
            pltpu.make_async_copy(key_ref.at[rows], keys.at[rows], sems.at[0, k]),
            pltpu.make_async_copy(value_ref.at[rows], values.at[rows], sems.at[1, k]),
        )

    def put(k):
        rows = pl.ds(k * size, size)
        return (
            pltpu.make_async_copy(turned.at[:, rows], turned_ref.at[:, rows], sems.at[2, k]),
            pltpu.make_async_copy(mixed.at[rows], mixed_ref.at[rows], sems.at[3, k]),
        )

    for k in range(chunks):
        for copy in fetch(k):
            copy.start()
    for k in range(chunks):
        for copy in fetch(k):
            copy.wait()
        rows = slice(k * size, (k + 1) * size)
        product = (keys[rows, :].astype(jnp.float32) * values[rows, :].astype(jnp.float32)).astype(jnp.bfloat16)
        mixed[rows, :] = product
        turned[:, rows] = product.T
        for copy in put(k):
            copy.start()
    for k in range(chunks):
        for copy in put(k):
            copy.wait()


def mix(key_gate, value_in):
    length, width = key_gate.shape
    chunks = length // LANES
    return pl.pallas_call(
        functools.partial(mix_kernel, chunks),
        in_specs=[pl.BlockSpec(memory_space=pl.ANY)] * 2,
        out_specs=[pl.BlockSpec(memory_space=pl.ANY)] * 2,
        out_shape=[
            jax.ShapeDtypeStruct((length, width), jnp.bfloat16),
            jax.ShapeDtypeStruct((width, length), jnp.bfloat16),
        ],
        scratch_shapes=[pltpu.VMEM((length, width), jnp.bfloat16)] * 3
        + [pltpu.VMEM((width, length), jnp.bfloat16), pltpu.SemaphoreType.DMA((4, chunks))],
        cost_estimate=pl.CostEstimate(flops=length * width, bytes_accessed=8 * length * width, transcendentals=0),
        name="mix",
    )(key_gate, value_in)


def taps_kernel(few, place_ref, taps_ref, out_ref, taps, out, sems):
    length = out_ref.shape[1]
    column = pl.multiple_of(place_ref[0] * LANES, LANES)

    def fetch(k):
        rows = pl.ds(k * length, length)
        return pltpu.make_async_copy(taps_ref.at[rows, pl.ds(column, LANES)], taps.at[rows], sems.at[k])

    for k in range(WIN):
        fetch(k).start()
    first = place_ref[1] * few
    rows = lax.broadcasted_iota(jnp.int32, (few, LANES), 0)
    lanes = lax.broadcasted_iota(jnp.int32, (few, LANES), 1)
    pick = (lanes == rows + first).astype(jnp.bfloat16)
    for k in range(WIN):
        fetch(k).wait()
        picked = lax.dot_general(
            pick,
            taps[k * length : (k + 1) * length, :].astype(jnp.bfloat16),
            (((1,), (1,)), ((), ())),
            preferred_element_type=jnp.float32,
        )
        out[k * few : (k + 1) * few, :] = picked.astype(jnp.bfloat16)
    put = pltpu.make_async_copy(out, out_ref.at[pl.ds(0, WIN * few)], sems.at[WIN])
    put.start()
    put.wait()


def turned_taps(place, filter_taps, few):
    length = filter_taps.shape[0] // WIN
    return pl.pallas_call(
        functools.partial(taps_kernel, few),
        grid_spec=pltpu.PrefetchScalarGridSpec(
            num_scalar_prefetch=1,
            in_specs=[pl.BlockSpec(memory_space=pl.ANY)],
            out_specs=pl.BlockSpec(memory_space=pl.ANY),
            scratch_shapes=[
                pltpu.VMEM((WIN * length, LANES), jnp.float32),
                pltpu.VMEM((WIN * few, length), jnp.bfloat16),
                pltpu.SemaphoreType.DMA((WIN + 1,)),
            ],
        ),
        out_shape=jax.ShapeDtypeStruct((length, length), jnp.bfloat16),
        cost_estimate=pl.CostEstimate(
            flops=2 * few * LANES * WIN * length, bytes_accessed=2 << 20, transcendentals=0
        ),
        name="turned_taps",
    )(place, filter_taps)


def conv_kernel(few, x_ref, taps_ref, table_ref, out_ref, rows, tap_rows, table, window, product, sems):
    tiles, length, pair = table_ref.shape
    count = x_ref.shape[0]
    spans = count // few

    copies = [
        pltpu.make_async_copy(x_ref, rows, sems.at[0]),
        pltpu.make_async_copy(taps_ref.at[pl.ds(0, WIN * few)], tap_rows, sems.at[1]),
        pltpu.make_async_copy(table_ref, table, sems.at[2]),
    ]
    for copy in copies:
        copy.start()
    for copy in copies:
        copy.wait()
    for tile in range(tiles):
        spectrum = jnp.dot(rows[...], table[tile], preferred_element_type=jnp.float32)
        taps = jnp.dot(tap_rows[...], table[tile], preferred_element_type=jnp.float32)
        sign = 1.0 if tile < tiles // 2 else -1.0
        for span in range(spans):
            now = slice(span * few, (span + 1) * few)
            window_real = sign * spectrum[now, LANES:]
            window_imag = -sign * spectrum[now, :LANES]
            if span > 0:
                before = slice((span - 1) * few, span * few)
                window_real = spectrum[before, :LANES] + window_real
                window_imag = spectrum[before, LANES:] + window_imag
            window[tile, 0, now, :] = window_real
            window[tile, 1, now, :] = window_imag
            window[tile, 2, now, :] = window_real + window_imag
        first, plus, minus = [], [], []
        for lag in range(WIN):
            h_real = (-sign / length) * taps[lag * few : (lag + 1) * few, :LANES]
            h_imag = (-sign / length) * taps[lag * few : (lag + 1) * few, LANES:]
            first.append(h_real)
            plus.append(h_real + h_imag)
            minus.append(h_imag - h_real)
        for low in range(0, few, 8):
            part = slice(low, low + 8)
            for span in range(spans):
                one = two = three = None
                for lag in range(min(WIN, span + 1)):
                    at = (span - lag) * few + low
                    term_one = first[lag][part] * window[tile, 2, at : at + 8, :]
                    term_two = plus[lag][part] * window[tile, 1, at : at + 8, :]
                    term_three = minus[lag][part] * window[tile, 0, at : at + 8, :]
                    one = term_one if one is None else one + term_one
                    two = term_two if two is None else two + term_two
                    three = term_three if three is None else three + term_three
                at = span * few + low
                product[tile, at : at + 8, :LANES] = (one + three).astype(jnp.bfloat16)
                product[tile, at : at + 8, LANES:] = (two - one).astype(jnp.bfloat16)
    total = None
    for tile in range(tiles):
        term = lax.dot_general(
            product[tile], table[tile], (((1,), (1,)), ((), ())), preferred_element_type=jnp.float32
        )
        total = term if total is None else total + term
    out_ref[...] = total.astype(jnp.bfloat16)


def convolve(turned, taps, table, few):
    count, length = turned.shape
    tiles, _, pair = table.shape
    return pl.pallas_call(
        functools.partial(conv_kernel, few),
        in_specs=[pl.BlockSpec(memory_space=pl.ANY)] * 3,
        out_specs=pl.BlockSpec(memory_space=pltpu.VMEM),
        out_shape=jax.ShapeDtypeStruct((count, length), jnp.bfloat16),
        scratch_shapes=[
            pltpu.VMEM((count, length), jnp.bfloat16),
            pltpu.VMEM((WIN * few, length), jnp.bfloat16),
            pltpu.VMEM(table.shape, jnp.bfloat16),
            pltpu.VMEM((tiles, 3, count, LANES), jnp.float32),
            pltpu.VMEM((tiles, count, pair), jnp.bfloat16),
            pltpu.SemaphoreType.DMA((3,)),
        ],
        compiler_params=pltpu.CompilerParams(vmem_limit_bytes=CONV_BYTES),
        cost_estimate=pl.CostEstimate(
            flops=4 * count * length * tiles * pair, bytes_accessed=3 << 20, transcendentals=0
        ),
        name="convolve",
    )(turned, taps, table)


def gate_kernel(conv_ref, mixed_ref, query_ref, skip_ref, gated_ref):
    conv = conv_ref[...].T.astype(jnp.float32)
    combined = conv + skip_ref[...] * mixed_ref[...].astype(jnp.float32)
    gated_ref[...] = (query_ref[...].astype(jnp.float32) * combined).astype(jnp.bfloat16)


def gate(conv_turned, mixed, query_gate, skip_gain):
    length, width = mixed.shape
    return pl.pallas_call(
        gate_kernel,
        out_shape=jax.ShapeDtypeStruct((length, width), jnp.bfloat16),
        compiler_params=PARAMS,
        cost_estimate=pl.CostEstimate(flops=4 * length * width, bytes_accessed=8 * length * width, transcendentals=0),
        name="gate",
    )(conv_turned, mixed, query_gate, skip_gain.reshape(1, width))


def weights_kernel(number, blocks_ref, weight_ref, own_ref, partner_ref, sems):
    width = weight_ref.shape[0]
    copies = []
    for k in range(number):
        for at, ref in enumerate((partner_ref, own_ref)):
            start = pl.multiple_of(blocks_ref[number * at + k] * width, width)
            copies.append(
                pltpu.make_async_copy(weight_ref.at[:, pl.ds(start, width)], ref.at[k], sems.at[number * at + k])
            )
    for copy in copies:
        copy.start()
    for copy in copies:
        copy.wait()


def weight_blocks(blocks, out_weight):
    width = out_weight.shape[0]
    number = blocks.shape[0] // 2
    shape = jax.ShapeDtypeStruct((number, width, width), jnp.bfloat16)
    return pl.pallas_call(
        functools.partial(weights_kernel, number),
        grid_spec=pltpu.PrefetchScalarGridSpec(
            num_scalar_prefetch=1,
            in_specs=[pl.BlockSpec(memory_space=pl.ANY)],
            out_specs=[pl.BlockSpec(memory_space=pltpu.VMEM)] * 2,
            scratch_shapes=[pltpu.SemaphoreType.DMA((2 * number,))],
        ),
        out_shape=[shape] * 2,
        cost_estimate=pl.CostEstimate(flops=0, bytes_accessed=8 << 20, transcendentals=0),
        name="weight_blocks",
    )(blocks, out_weight)


def own_part_kernel(number, gated_ref, weight_ref, out_ref):
    for k in range(number):
        out_ref[k] = jnp.dot(gated_ref[...], weight_ref[k], preferred_element_type=jnp.float32)


def own_part(gated, own_weight):
    length, width = gated.shape
    number = own_weight.shape[0]
    return pl.pallas_call(
        functools.partial(own_part_kernel, number),
        in_specs=[pl.BlockSpec(memory_space=pltpu.VMEM)] * 2,
        out_specs=pl.BlockSpec(memory_space=pltpu.VMEM),
        out_shape=jax.ShapeDtypeStruct((number, length, width), jnp.float32),
        compiler_params=PARAMS,
        cost_estimate=pl.CostEstimate(
            flops=2 * length * width * width * number, bytes_accessed=2 << 20, transcendentals=0
        ),
        name="own_part",
    )(gated, own_weight)


def project_kernel(which, part_ref, other_ref, weight_ref, *outs):
    half = other_ref.shape[0] // 2
    for at, k in enumerate(which):
        total = part_ref[k] + jnp.dot(other_ref[...], weight_ref[k], preferred_element_type=jnp.float32)
        total = total.astype(jnp.bfloat16)
        outs[2 * at][...] = total[:half]
        outs[2 * at + 1][...] = total[half:]


def project(which, part, other, other_weight):
    _, length, width = part.shape
    number = len(which)
    return pl.pallas_call(
        functools.partial(project_kernel, which),
        in_specs=[pl.BlockSpec(memory_space=pltpu.VMEM)] * 3,
        out_specs=[pl.BlockSpec(memory_space=pltpu.VMEM)] * (2 * number),
        out_shape=[jax.ShapeDtypeStruct((length // 2, width), jnp.bfloat16)] * (2 * number),
        compiler_params=PARAMS,
        cost_estimate=pl.CostEstimate(
            flops=2 * length * width * width * number, bytes_accessed=number << 20, transcendentals=0
        ),
        name="project",
    )(part, other, other_weight)


def finish_kernel(first, one_ref, two_ref, three_ref, *refs):
    out_ref, out, sems = refs[-3:]
    half = one_ref.shape[0]
    size = half // 2
    base = 0 if first else half

    def put(k):
        part = pl.ds(k * size, size)
        return pltpu.make_async_copy(out.at[part], out_ref.at[pl.ds(base + k * size, size)], sems.at[k])

    for k in range(2):
        rows = slice(k * size, (k + 1) * size)
        total = sum(ref[rows, :].astype(jnp.float32) for ref in (one_ref, two_ref, three_ref))
        out[rows, :] = total.astype(jnp.bfloat16)
        put(k).start()
    for k in range(2):
        put(k).wait()


def finish(terms, into=None):
    half, width = terms[0].shape
    first = into is None
    return pl.pallas_call(
        functools.partial(finish_kernel, first),
        in_specs=[pl.BlockSpec(memory_space=pltpu.VMEM)] * 3 + [pl.BlockSpec(memory_space=pl.ANY)] * (not first),
        out_specs=pl.BlockSpec(memory_space=pl.ANY),
        out_shape=jax.ShapeDtypeStruct((2 * half, width), jnp.bfloat16),
        scratch_shapes=[pltpu.VMEM((half, width), jnp.bfloat16), pltpu.SemaphoreType.DMA((2,))],
        input_output_aliases={} if first else {3: 0},
        compiler_params=PARAMS,
        cost_estimate=pl.CostEstimate(flops=3 * half * width, bytes_accessed=8 * half * width, transcendentals=0),
        name="finish",
    )(*terms, *([] if first else [into]))


def added(one, two):
    return (one.astype(jnp.float32) + two.astype(jnp.float32)).astype(jnp.bfloat16)


def body(query_gate, key_gate, value_in, filter_taps, skip_gain, out_weight):
    length, width = query_gate.shape
    ctx, groups = lax.axis_size("ctx"), lax.axis_size("ch")
    ring = groups // CORES
    few = width // ctx
    here, group = lax.axis_index("ctx"), lax.axis_index("ch")
    y, core = group // CORES, group % CORES
    per_tile = LANES // few
    table = jnp.asarray(odd_tables(length))

    def ch_shift(block, dy, dcore):
        route = [(i, ((i // CORES + dy) % ring) * CORES + (i % CORES + dcore) % CORES) for i in range(groups)]
        return lax.ppermute(block, "ch", route)

    mixed, turned = mix(key_gate, value_in)
    place = jnp.stack([here // per_tile, here % per_tile]).astype(jnp.int32)
    taps = turned_taps(place, filter_taps, few)
    ahead = [(y + step) % ring for step in (2, 1, 3, 0)]
    blocks = jnp.stack([k * CORES + at for at in (1 - core, core) for k in ahead]).astype(jnp.int32)
    own_weight, partner_weight = weight_blocks(blocks, out_weight)
    other_weight = ch_shift(partner_weight, 0, 1)

    long_rows = lax.all_to_all(turned.reshape(ctx, few, length), "ctx", 0, 0)
    conv_rows = convolve(long_rows.reshape(ctx * few, length), taps, table, few)
    conv_turned = lax.all_to_all(conv_rows.reshape(ctx, few, length), "ctx", 0, 0).reshape(width, length)

    gated = gate(conv_turned, mixed, query_gate, skip_gain)
    other = ch_shift(gated, 0, 1)
    part = own_part(gated, own_weight)
    across_low, across_high = project((0,), part, other, other_weight)
    got_low = ch_shift(across_low, 1, 0)
    up_low, up_high, down_low, down_high, own_low, own_high = project((1, 2, 3), part, other, other_weight)
    across_high, up_high = lax.optimization_barrier((across_high, up_high))
    got_high = ch_shift(across_high, -1, 0)
    from_below_high = ch_shift(up_high, 1, 0)
    from_above_low = ch_shift(down_low, -1, 0)
    from_below_low = ch_shift(added(up_low, got_low), 1, 0)
    from_above_high = ch_shift(added(down_high, got_high), -1, 0)
    lower = finish((own_low, from_above_low, from_below_low))
    return finish((own_high, from_below_high, from_above_high), lower)


def solution(mesh):
    in_specs = (
        P("ctx", "ch"),
        P("ctx", "ch"),
        P("ctx", "ch"),
        P(None, "ch"),
        P("ch"),
        P("ch", None),
    )
    out_specs = P("ctx", "ch")
    return jax.shard_map(body, mesh=mesh, in_specs=in_specs, out_specs=out_specs, check_vma=False)
```

```python
import functools

import jax
import jax.numpy as jnp
import numpy as np
from jax import lax
from jax.experimental import pallas as pl
from jax.experimental.pallas import tpu as pltpu
from jax.sharding import PartitionSpec as P

WIN = 8
LANES = 128
CORES = 2
CONV_BYTES = 54400 << 10
PARAMS = pltpu.CompilerParams(vmem_limit_bytes=20 << 20)


def odd_tables(length):
    order = np.concatenate([np.arange(0, length, 2), np.arange(1, length, 2)])
    turns = (np.arange(length)[:, None] * (2 * order[None, :] + 1)) % (4 * length)
    angle = turns * (np.pi / (2 * length))
    tiles = length // LANES
    cos_part = np.cos(angle).reshape(length, tiles, LANES)
    sin_part = -np.sin(angle).reshape(length, tiles, LANES)
    table = np.concatenate([cos_part, sin_part], axis=2).transpose(1, 0, 2)
    return table.astype(jnp.bfloat16)


def mix_kernel(chunks, key_ref, value_ref, mixed_ref, turned_ref, keys, values, mixed, turned, sems):
    size = key_ref.shape[0] // chunks

    def fetch(k):
        rows = pl.ds(k * size, size)
        return (
            pltpu.make_async_copy(key_ref.at[rows], keys.at[rows], sems.at[0, k]),
            pltpu.make_async_copy(value_ref.at[rows], values.at[rows], sems.at[1, k]),
        )

    def put(k):
        rows = pl.ds(k * size, size)
        return (
            pltpu.make_async_copy(turned.at[:, rows], turned_ref.at[:, rows], sems.at[2, k]),
            pltpu.make_async_copy(mixed.at[rows], mixed_ref.at[rows], sems.at[3, k]),
        )

    for k in range(chunks):
        for copy in fetch(k):
            copy.start()
    for k in range(chunks):
        for copy in fetch(k):
            copy.wait()
        rows = slice(k * size, (k + 1) * size)
        product = (keys[rows, :].astype(jnp.float32) * values[rows, :].astype(jnp.float32)).astype(jnp.bfloat16)
        mixed[rows, :] = product
        turned[:, rows] = product.T
        for copy in put(k):
            copy.start()
    for k in range(chunks):
        for copy in put(k):
            copy.wait()


def mix(key_gate, value_in):
    length, width = key_gate.shape
    chunks = length // LANES
    return pl.pallas_call(
        functools.partial(mix_kernel, chunks),
        in_specs=[pl.BlockSpec(memory_space=pl.ANY)] * 2,
        out_specs=[pl.BlockSpec(memory_space=pl.ANY)] * 2,
        out_shape=[
            jax.ShapeDtypeStruct((length, width), jnp.bfloat16),
            jax.ShapeDtypeStruct((width, length), jnp.bfloat16),
        ],
        scratch_shapes=[pltpu.VMEM((length, width), jnp.bfloat16)] * 3
        + [pltpu.VMEM((width, length), jnp.bfloat16), pltpu.SemaphoreType.DMA((4, chunks))],
        cost_estimate=pl.CostEstimate(flops=length * width, bytes_accessed=8 * length * width, transcendentals=0),
        name="mix",
    )(key_gate, value_in)


def taps_kernel(few, place_ref, taps_ref, out_ref, taps, out, sems):
    length = out_ref.shape[1]
    column = pl.multiple_of(place_ref[0] * LANES, LANES)

    def fetch(k):
        rows = pl.ds(k * length, length)
        return pltpu.make_async_copy(taps_ref.at[rows, pl.ds(column, LANES)], taps.at[rows], sems.at[k])

    for k in range(WIN):
        fetch(k).start()
    first = place_ref[1] * few
    rows = lax.broadcasted_iota(jnp.int32, (few, LANES), 0)
    lanes = lax.broadcasted_iota(jnp.int32, (few, LANES), 1)
    pick = (lanes == rows + first).astype(jnp.bfloat16)
    for k in range(WIN):
        fetch(k).wait()
        picked = lax.dot_general(
            pick,
            taps[k * length : (k + 1) * length, :].astype(jnp.bfloat16),
            (((1,), (1,)), ((), ())),
            preferred_element_type=jnp.float32,
        )
        out[k * few : (k + 1) * few, :] = picked.astype(jnp.bfloat16)
    put = pltpu.make_async_copy(out, out_ref.at[pl.ds(0, WIN * few)], sems.at[WIN])
    put.start()
    put.wait()


def turned_taps(place, filter_taps, few):
    length = filter_taps.shape[0] // WIN
    return pl.pallas_call(
        functools.partial(taps_kernel, few),
        grid_spec=pltpu.PrefetchScalarGridSpec(
            num_scalar_prefetch=1,
            in_specs=[pl.BlockSpec(memory_space=pl.ANY)],
            out_specs=pl.BlockSpec(memory_space=pl.ANY),
            scratch_shapes=[
                pltpu.VMEM((WIN * length, LANES), jnp.float32),
                pltpu.VMEM((WIN * few, length), jnp.bfloat16),
                pltpu.SemaphoreType.DMA((WIN + 1,)),
            ],
        ),
        out_shape=jax.ShapeDtypeStruct((length, length), jnp.bfloat16),
        cost_estimate=pl.CostEstimate(
            flops=2 * few * LANES * WIN * length, bytes_accessed=2 << 20, transcendentals=0
        ),
        name="turned_taps",
    )(place, filter_taps)


def conv_kernel(few, x_ref, taps_ref, table_ref, out_ref, rows, tap_rows, table, window, product, sems):
    tiles, length, pair = table_ref.shape
    count = x_ref.shape[0]
    spans = count // few

    copies = [
        pltpu.make_async_copy(x_ref, rows, sems.at[0]),
        pltpu.make_async_copy(taps_ref.at[pl.ds(0, WIN * few)], tap_rows, sems.at[1]),
        pltpu.make_async_copy(table_ref.at[pl.ds(0, tiles // 2)], table.at[pl.ds(0, tiles // 2)], sems.at[2]),
        pltpu.make_async_copy(
            table_ref.at[pl.ds(tiles // 2, tiles // 2)], table.at[pl.ds(tiles // 2, tiles // 2)], sems.at[3]
        ),
    ]
    for copy in copies:
        copy.start()
    for copy in copies[:3]:
        copy.wait()
    for tile in range(tiles):
        if tile == tiles // 2:
            copies[3].wait()
        spectrum = jnp.dot(rows[...], table[tile], preferred_element_type=jnp.float32)
        taps = jnp.dot(tap_rows[...], table[tile], preferred_element_type=jnp.float32)
        sign = 1.0 if tile < tiles // 2 else -1.0
        for span in range(spans):
            now = slice(span * few, (span + 1) * few)
            window_real = sign * spectrum[now, LANES:]
            window_imag = -sign * spectrum[now, :LANES]
            if span > 0:
                before = slice((span - 1) * few, span * few)
                window_real = spectrum[before, :LANES] + window_real
                window_imag = spectrum[before, LANES:] + window_imag
            window[tile, 0, now, :] = window_real
            window[tile, 1, now, :] = window_imag
            window[tile, 2, now, :] = window_real + window_imag
        first, plus, minus = [], [], []
        for lag in range(WIN):
            h_real = (-sign / length) * taps[lag * few : (lag + 1) * few, :LANES]
            h_imag = (-sign / length) * taps[lag * few : (lag + 1) * few, LANES:]
            first.append(h_real)
            plus.append(h_real + h_imag)
            minus.append(h_imag - h_real)
        for low in range(0, few, 8):
            part = slice(low, low + 8)
            for span in range(spans):
                one = two = three = None
                for lag in range(min(WIN, span + 1)):
                    at = (span - lag) * few + low
                    term_one = first[lag][part] * window[tile, 2, at : at + 8, :]
                    term_two = plus[lag][part] * window[tile, 1, at : at + 8, :]
                    term_three = minus[lag][part] * window[tile, 0, at : at + 8, :]
                    one = term_one if one is None else one + term_one
                    two = term_two if two is None else two + term_two
                    three = term_three if three is None else three + term_three
                at = span * few + low
                product[tile, at : at + 8, :LANES] = (one + three).astype(jnp.bfloat16)
                product[tile, at : at + 8, LANES:] = (two - one).astype(jnp.bfloat16)
    total = None
    for tile in range(tiles):
        term = lax.dot_general(
            product[tile], table[tile], (((1,), (1,)), ((), ())), preferred_element_type=jnp.float32
        )
        total = term if total is None else total + term
    out_ref[...] = total.astype(jnp.bfloat16)


def convolve(turned, taps, table, few):
    count, length = turned.shape
    tiles, _, pair = table.shape
    return pl.pallas_call(
        functools.partial(conv_kernel, few),
        in_specs=[pl.BlockSpec(memory_space=pl.ANY)] * 3,
        out_specs=pl.BlockSpec(memory_space=pltpu.VMEM),
        out_shape=jax.ShapeDtypeStruct((count, length), jnp.bfloat16),
        scratch_shapes=[
            pltpu.VMEM((count, length), jnp.bfloat16),
            pltpu.VMEM((WIN * few, length), jnp.bfloat16),
            pltpu.VMEM(table.shape, jnp.bfloat16),
            pltpu.VMEM((tiles, 3, count, LANES), jnp.float32),
            pltpu.VMEM((tiles, count, pair), jnp.bfloat16),
            pltpu.SemaphoreType.DMA((4,)),
        ],
        compiler_params=pltpu.CompilerParams(vmem_limit_bytes=CONV_BYTES),
        cost_estimate=pl.CostEstimate(
            flops=4 * count * length * tiles * pair, bytes_accessed=3 << 20, transcendentals=0
        ),
        name="convolve",
    )(turned, taps, table)


def gate_kernel(conv_ref, mixed_ref, query_ref, skip_ref, gated_ref):
    conv = conv_ref[...].T.astype(jnp.float32)
    combined = conv + skip_ref[...] * mixed_ref[...].astype(jnp.float32)
    gated_ref[...] = (query_ref[...].astype(jnp.float32) * combined).astype(jnp.bfloat16)


def gate(conv_turned, mixed, query_gate, skip_gain):
    length, width = mixed.shape
    return pl.pallas_call(
        gate_kernel,
        out_shape=jax.ShapeDtypeStruct((length, width), jnp.bfloat16),
        compiler_params=PARAMS,
        cost_estimate=pl.CostEstimate(flops=4 * length * width, bytes_accessed=8 * length * width, transcendentals=0),
        name="gate",
    )(conv_turned, mixed, query_gate, skip_gain.reshape(1, width))


def weights_kernel(number, blocks_ref, weight_ref, own_ref, partner_ref, sems):
    width = weight_ref.shape[0]
    copies = []
    for k in range(number):
        for at, ref in enumerate((partner_ref, own_ref)):
            start = pl.multiple_of(blocks_ref[number * at + k] * width, width)
            copies.append(
                pltpu.make_async_copy(weight_ref.at[:, pl.ds(start, width)], ref.at[k], sems.at[number * at + k])
            )
    for copy in copies:
        copy.start()
    for copy in copies:
        copy.wait()


def weight_blocks(blocks, out_weight):
    width = out_weight.shape[0]
    number = blocks.shape[0] // 2
    shape = jax.ShapeDtypeStruct((number, width, width), jnp.bfloat16)
    return pl.pallas_call(
        functools.partial(weights_kernel, number),
        grid_spec=pltpu.PrefetchScalarGridSpec(
            num_scalar_prefetch=1,
            in_specs=[pl.BlockSpec(memory_space=pl.ANY)],
            out_specs=[pl.BlockSpec(memory_space=pltpu.VMEM)] * 2,
            scratch_shapes=[pltpu.SemaphoreType.DMA((2 * number,))],
        ),
        out_shape=[shape] * 2,
        cost_estimate=pl.CostEstimate(flops=0, bytes_accessed=8 << 20, transcendentals=0),
        name="weight_blocks",
    )(blocks, out_weight)


def own_part_kernel(number, gated_ref, weight_ref, out_ref):
    for k in range(number):
        out_ref[k] = jnp.dot(gated_ref[...], weight_ref[k], preferred_element_type=jnp.float32)


def own_part(gated, own_weight):
    length, width = gated.shape
    number = own_weight.shape[0]
    return pl.pallas_call(
        functools.partial(own_part_kernel, number),
        in_specs=[pl.BlockSpec(memory_space=pltpu.VMEM)] * 2,
        out_specs=pl.BlockSpec(memory_space=pltpu.VMEM),
        out_shape=jax.ShapeDtypeStruct((number, length, width), jnp.float32),
        compiler_params=PARAMS,
        cost_estimate=pl.CostEstimate(
            flops=2 * length * width * width * number, bytes_accessed=2 << 20, transcendentals=0
        ),
        name="own_part",
    )(gated, own_weight)


def project_kernel(which, part_ref, other_ref, weight_ref, *outs):
    half = other_ref.shape[0] // 2
    for at, k in enumerate(which):
        total = part_ref[k] + jnp.dot(other_ref[...], weight_ref[k], preferred_element_type=jnp.float32)
        total = total.astype(jnp.bfloat16)
        outs[2 * at][...] = total[:half]
        outs[2 * at + 1][...] = total[half:]


def project(which, part, other, other_weight):
    _, length, width = part.shape
    number = len(which)
    return pl.pallas_call(
        functools.partial(project_kernel, which),
        in_specs=[pl.BlockSpec(memory_space=pltpu.VMEM)] * 3,
        out_specs=[pl.BlockSpec(memory_space=pltpu.VMEM)] * (2 * number),
        out_shape=[jax.ShapeDtypeStruct((length // 2, width), jnp.bfloat16)] * (2 * number),
        compiler_params=PARAMS,
        cost_estimate=pl.CostEstimate(
            flops=2 * length * width * width * number, bytes_accessed=number << 20, transcendentals=0
        ),
        name="project",
    )(part, other, other_weight)


def finish_kernel(first, one_ref, two_ref, three_ref, *refs):
    out_ref, out, sems = refs[-3:]
    half = one_ref.shape[0]
    size = half // 2
    base = 0 if first else half

    def put(k):
        part = pl.ds(k * size, size)
        return pltpu.make_async_copy(out.at[part], out_ref.at[pl.ds(base + k * size, size)], sems.at[k])

    for k in range(2):
        rows = slice(k * size, (k + 1) * size)
        total = sum(ref[rows, :].astype(jnp.float32) for ref in (one_ref, two_ref, three_ref))
        out[rows, :] = total.astype(jnp.bfloat16)
        put(k).start()
    for k in range(2):
        put(k).wait()


def finish(terms, into=None):
    half, width = terms[0].shape
    first = into is None
    return pl.pallas_call(
        functools.partial(finish_kernel, first),
        in_specs=[pl.BlockSpec(memory_space=pltpu.VMEM)] * 3 + [pl.BlockSpec(memory_space=pl.ANY)] * (not first),
        out_specs=pl.BlockSpec(memory_space=pl.ANY),
        out_shape=jax.ShapeDtypeStruct((2 * half, width), jnp.bfloat16),
        scratch_shapes=[pltpu.VMEM((half, width), jnp.bfloat16), pltpu.SemaphoreType.DMA((2,))],
        input_output_aliases={} if first else {3: 0},
        compiler_params=PARAMS,
        cost_estimate=pl.CostEstimate(flops=3 * half * width, bytes_accessed=8 * half * width, transcendentals=0),
        name="finish",
    )(*terms, *([] if first else [into]))


def added(one, two):
    return (one.astype(jnp.float32) + two.astype(jnp.float32)).astype(jnp.bfloat16)


def body(query_gate, key_gate, value_in, filter_taps, skip_gain, out_weight):
    length, width = query_gate.shape
    ctx, groups = lax.axis_size("ctx"), lax.axis_size("ch")
    ring = groups // CORES
    few = width // ctx
    here, group = lax.axis_index("ctx"), lax.axis_index("ch")
    y, core = group // CORES, group % CORES
    per_tile = LANES // few
    table = jnp.asarray(odd_tables(length))

    def ch_shift(block, dy, dcore):
        route = [(i, ((i // CORES + dy) % ring) * CORES + (i % CORES + dcore) % CORES) for i in range(groups)]
        return lax.ppermute(block, "ch", route)

    mixed, turned = mix(key_gate, value_in)
    place = jnp.stack([here // per_tile, here % per_tile]).astype(jnp.int32)
    taps = turned_taps(place, filter_taps, few)
    ahead = [(y + step) % ring for step in (2, 1, 3, 0)]
    blocks = jnp.stack([k * CORES + at for at in (1 - core, core) for k in ahead]).astype(jnp.int32)
    own_weight, partner_weight = weight_blocks(blocks, out_weight)
    other_weight = ch_shift(partner_weight, 0, 1)

    long_rows = lax.all_to_all(turned.reshape(ctx, few, length), "ctx", 0, 0)
    conv_rows = convolve(long_rows.reshape(ctx * few, length), taps, table, few)
    conv_turned = lax.all_to_all(conv_rows.reshape(ctx, few, length), "ctx", 0, 0).reshape(width, length)

    gated = gate(conv_turned, mixed, query_gate, skip_gain)
    other = ch_shift(gated, 0, 1)
    part = own_part(gated, own_weight)
    across_low, across_high = project((0,), part, other, other_weight)
    got_low = ch_shift(across_low, 1, 0)
    up_low, up_high, down_low, down_high, own_low, own_high = project((1, 2, 3), part, other, other_weight)
    across_high, up_high = lax.optimization_barrier((across_high, up_high))
    got_high = ch_shift(across_high, -1, 0)
    from_below_high = ch_shift(up_high, 1, 0)
    from_above_low = ch_shift(down_low, -1, 0)
    from_below_low = ch_shift(added(up_low, got_low), 1, 0)
    from_above_high = ch_shift(added(down_high, got_high), -1, 0)
    lower = finish((own_low, from_above_low, from_below_low))
    return finish((own_high, from_below_high, from_above_high), lower)


def solution(mesh):
    in_specs = (
        P("ctx", "ch"),
        P("ctx", "ch"),
        P("ctx", "ch"),
        P(None, "ch"),
        P("ch"),
        P("ch", None),
    )
    out_specs = P("ctx", "ch")
    return jax.shard_map(body, mesh=mesh, in_specs=in_specs, out_specs=out_specs, check_vma=False)
```
